32 devices in a mesh: row: 4 (over y, x), col: 8 (over z, core).
Axes of the slice: x: 2, y: 2, z: 4, core: 2. Of those that a mesh axis runs over, the one named last changes fastest.
Arguments:
- activations: bfloat16 [256, 16384], P(None, 'row'), may hold values from -3 to 3
- cotangent: bfloat16 [256, 16384], P(None, 'row'), may hold values from -0.59765625 to 0.59765625
- forget: int32 [256], replicated, may hold values 0 or 1
- lengths: int32 [4, 4], P('row'), may hold values from 1 to 32, 64 in all within a row
- query_weight: bfloat16 [16384, 8192], P('row', 'col'), may hold values from -0.046875 to 0.046875
- key_weight: bfloat16 [16384, 512], P('row'), may hold values from -0.046875 to 0.046875
- value_weight: bfloat16 [16384, 512], P('row'), may hold values from -0.046875 to 0.046875
- output_projection_weight: bfloat16 [8192, 16384], P('col', 'row'), may hold values from -0.0625 to 0.0625
- query_down: bfloat16 [16384, 32], P('row'), may hold values from -0.046875 to 0.046875
- query_up: bfloat16 [32, 8192], P(None, 'col'), may hold values from -1 to 1
- output_down: bfloat16 [8192, 32], P('col'), may hold values from -0.0625 to 0.0625
- output_up: bfloat16 [32, 16384], P(None, 'row'), may hold values from -1 to 1
Outputs:
- query_down_gradient: float32 [16384, 32], P('row')
- query_up_gradient: float32 [32, 8192], P(None, 'col')
- output_down_gradient: float32 [8192, 32], P('col')
- output_up_gradient: float32 [32, 16384], P(None, 'row')
The draws below stay inside these ranges and needn't reach their ends.
Inputs may be any that keep to these rules, and one draw needn't show every extreme that they name: In every row of lengths the 4 values sum to 64, and the largest is exactly 32.
All inputs are finite; a program needn't handle non-finite values.
Results may differ from the reference program's by a relative error of at most 0.025.
Values may be sent and summed in bfloat16 or wider, within the bound.
A program may use at most 128 MiB of HBM per device.

```python
import math
import jax
import jax.numpy as jnp
import numpy as np
from jax import lax

D = 16384
HD = 128
HEADS = 64
KVH = 4
RANK = 32
SEGS = 4
TOK_BLK = 64
MOST = 32
TOKENS = 256
N_ROW = 4


def set_ends(values, stream_key, smallest, high):
    spot = [jax.random.randint(jax.random.fold_in(stream_key, axis), (), 0, length) for axis, length in enumerate(values.shape)]
    widest = values.shape.index(max(values.shape))
    next_to = spot[:widest] + [(spot[widest] + 1) % values.shape[widest]] + spot[widest + 1:]
    return values.at[tuple(spot)].set(smallest).at[tuple(next_to)].set(high)


def shard_levels(key, extent, cuts, smallest, largest):
    def one(dim, shards_of):
        steps = jax.random.uniform(jax.random.fold_in(jax.random.fold_in(key, 6), dim), (shards_of,), jnp.float32, smallest / len(cuts), largest / len(cuts))
        return jnp.repeat(jnp.exp(steps), extent[dim] // shards_of).reshape((-1,) + (1,) * (len(extent) - dim - 1))

    gain = one(*cuts[0])
    for cut in cuts[1:]:
        gain = gain * one(*cut)
    return gain


def profile(number_of, total, most, skew):
    portions = [(1 << 20) // math.isqrt(rank ** skew) + 1 for rank in range(2, number_of + 1)]
    spare, holding = total - most - (number_of - 1), [1] * (number_of - 1)
    while spare > 0:
        movable = [i for i in range(number_of - 1) if holding[i] < most]
        whole, budget = sum([portions[i] for i in movable]), spare
        for i in movable:
            addition = min(most - holding[i], max(1, budget * portions[i] // whole), spare)
            holding[i] = holding[i] + addition
            spare = spare - addition
    return np.array([most] + holding)


def ragged(key, amount, total, reach, lean):
    if amount == 2:
        one = jax.random.randint(key, (), max(1, total - reach), min(reach, total - 1) + 1)
        return jnp.stack([one, total - one])
    sizes = jnp.asarray(profile(amount, total, reach, lean), jnp.int32)
    couples = (amount - 1) // 2
    giver, receiver = sizes[1:1 + 2 * couples:2], sizes[2:2 + 2 * couples:2]
    slack = jnp.minimum(giver - 1, reach - receiver)
    passed = jax.random.randint(jax.random.fold_in(key, 1), (couples,), 0, 1 << 20) % (slack + 1)
    sizes = sizes.at[1:1 + 2 * couples:2].set(giver - passed).at[2:2 + 2 * couples:2].set(receiver + passed)
    return sizes[jax.random.permutation(jax.random.fold_in(key, 2), amount)]


def noise(stream_key, extent, deviation, reach, shards=(), held_as=jnp.bfloat16):
    result = jax.random.normal(stream_key, extent, jnp.float32) * deviation
    if len(shards) > 0:
        result = shard_levels(stream_key, extent, shards, -0.22, 0.18) * result
    return jnp.clip(result, min=-reach, max=reach).astype(held_as)


def setup_inputs(seed: int = 0) -> dict:
    streams_of = jax.random.split(jax.random.key(seed), 13)
    activations = noise(streams_of[0], (TOKENS, D), 1.0, 3.0, ((1, 4),))
    cotangent = noise(streams_of[1], (TOKENS, D), 0.1, 0.59765625, ((1, 4),))
    forget = set_ends((jax.random.randint(streams_of[2], (TOKENS,), 0, 4) < 1).astype(jnp.int32), jax.random.fold_in(streams_of[2], 1), 0, 1)
    lengths = jax.vmap(lambda own: ragged(own, SEGS, TOK_BLK, MOST, 1))(jax.random.split(streams_of[3], N_ROW)).reshape((N_ROW, SEGS)).astype(jnp.int32)
    query_weight = noise(streams_of[4], (D, HEADS * HD), D ** -0.5, 0.046875, ((0, 4), (1, 8)))
    key_weight = noise(streams_of[5], (D, KVH * HD), D ** -0.5, 0.046875, ((0, 4),))
    value_weight = noise(streams_of[6], (D, KVH * HD), D ** -0.5, 0.046875, ((0, 4),))
    output_projection_weight = noise(streams_of[7], (HEADS * HD, D), (HEADS * HD) ** -0.5, 0.0625, ((0, 8), (1, 4)))
    query_down = noise(streams_of[8], (D, RANK), D ** -0.5, 0.046875, ((0, 4),))
    query_up = noise(streams_of[9], (RANK, HEADS * HD), RANK ** -0.5, 1.0, ((1, 8),))
    output_down = noise(streams_of[10], (HEADS * HD, RANK), (HEADS * HD) ** -0.5, 0.0625, ((0, 8),))
    output_up = noise(streams_of[11], (RANK, D), RANK ** -0.5, 1.0, ((1, 4),))
    return dict(activations=activations, cotangent=cotangent, forget=forget, lengths=lengths, query_weight=query_weight, key_weight=key_weight, value_weight=value_weight, output_projection_weight=output_projection_weight, query_down=query_down, query_up=query_up, output_down=output_down, output_up=output_up)


adapter_scale = 0.5
highest_precision = lax.Precision.HIGHEST

def to_bf16(value):
    return lax.optimization_barrier(value.astype(jnp.bfloat16))

def rounded_sum(term_fn, shape):

    def add_block(total, block):
        term = to_bf16(term_fn(block))
        return (total + term.astype(jnp.float32), None)
    total, _ = lax.scan(add_block, jnp.zeros(shape, jnp.float32), jnp.arange(N_ROW, dtype=jnp.int32))
    return total

def reference(activations, cotangent, forget, lengths, query_weight, key_weight, value_weight, output_projection_weight, query_down, query_up, output_down, output_up):
    block_width = D // N_ROW
    query_cols = HEADS * HD
    kv_cols = KVH * HD
    group_size = HEADS // KVH
    up_projection_broad = query_up.astype(jnp.float32)
    down_projection_broad = output_down.astype(jnp.float32)
    inverse = 1.0 / math.sqrt(HD)

    def forward_part(block):
        first_col = (block * block_width).astype(jnp.int32)
        inputs = lax.dynamic_slice_in_dim(activations, first_col, block_width, 1)
        reduced_result = jnp.dot(inputs, lax.dynamic_slice_in_dim(query_down, first_col, block_width, 0), preferred_element_type=jnp.float32)
        query_partial_term = jnp.dot(inputs, lax.dynamic_slice_in_dim(query_weight, first_col, block_width, 0), preferred_element_type=jnp.float32)
        query_partial_term = query_partial_term + adapter_scale * jnp.dot(reduced_result, up_projection_broad, precision=highest_precision)
        key_term = jnp.dot(inputs, lax.dynamic_slice_in_dim(key_weight, first_col, block_width, 0), preferred_element_type=jnp.float32)
        value_term = jnp.dot(inputs, lax.dynamic_slice_in_dim(value_weight, first_col, block_width, 0), preferred_element_type=jnp.float32)
        return jnp.concatenate([query_partial_term, key_term, value_term, reduced_result], axis=1)
    summed = rounded_sum(forward_part, (TOKENS, query_cols + 2 * kv_cols + RANK))
    query_rows = to_bf16(summed[:, :query_cols]).astype(jnp.float32)
    key_rows = to_bf16(summed[:, query_cols:query_cols + kv_cols]).astype(jnp.float32)
    value_rows = to_bf16(summed[:, query_cols + kv_cols:query_cols + 2 * kv_cols]).astype(jnp.float32)
    input_lowrank_factor = summed[:, query_cols + 2 * kv_cols:]
    query_heads = query_rows.reshape(N_ROW, TOK_BLK, HEADS, HD)
    key_heads = jnp.repeat(key_rows.reshape(N_ROW, TOK_BLK, KVH, HD), group_size, axis=2)
    value_heads = jnp.repeat(value_rows.reshape(N_ROW, TOK_BLK, KVH, HD), group_size, axis=2)
    seg_ends = jnp.cumsum(lengths, axis=1).astype(jnp.int32)
    position = jnp.arange(TOK_BLK, dtype=jnp.int32)
    segment = lax.optimization_barrier(jnp.sum((position[None, :, None] >= seg_ends[:, None, :]).astype(jnp.int32), axis=2))
    allowed = (segment[:, :, None] == segment[:, None, :]) & (position[None, None, :] <= position[None, :, None])
    scores = jnp.einsum('bqhd,bkhd->bhqk', query_heads, key_heads, precision=highest_precision) * inverse
    numerator = jnp.where(allowed[:, None], jnp.exp(scores), 0.0)
    softmax = numerator / lax.optimization_barrier(jnp.sum(numerator, axis=3, keepdims=True))
    weights = to_bf16(softmax).astype(jnp.float32)
    hidden_state = jnp.einsum('bhqk,bkhd->bqhd', weights, value_heads, precision=highest_precision).reshape(TOKENS, query_cols)
    hidden_state = to_bf16(hidden_state)
    sign_flip = (1 - 2 * forget).astype(jnp.bfloat16)
    output_gradient = cotangent * sign_flip[:, None]

    def backward_part(block):
        first_col = (block * block_width).astype(jnp.int32)
        grads = lax.dynamic_slice_in_dim(output_gradient, first_col, block_width, 1)
        reduced_result = jnp.dot(grads, lax.dynamic_slice_in_dim(output_up, first_col, block_width, 1).T, preferred_element_type=jnp.float32)
        hidden_state_term = jnp.dot(grads, lax.dynamic_slice_in_dim(output_projection_weight, first_col, block_width, 1).T, preferred_element_type=jnp.float32)
        hidden_state_term = hidden_state_term + adapter_scale * jnp.dot(reduced_result, down_projection_broad.T, precision=highest_precision)
        return jnp.concatenate([hidden_state_term, reduced_result], axis=1)
    backward = rounded_sum(backward_part, (TOKENS, query_cols + RANK))
    hidden_grad = to_bf16(backward[:, :query_cols]).astype(jnp.float32).reshape(N_ROW, TOK_BLK, HEADS, HD)
    gradient_lowrank_factor = backward[:, query_cols:]
    prob_grad = jnp.einsum('bqhd,bkhd->bhqk', hidden_grad, value_heads, precision=highest_precision)
    score_grad = softmax * (prob_grad - lax.optimization_barrier(jnp.sum(prob_grad * softmax, axis=3, keepdims=True)))
    query_gradient = (jnp.einsum('bhqk,bkhd->bqhd', score_grad, key_heads, precision=highest_precision) * inverse).reshape(TOKENS, query_cols)
    query_lowrank_factor = to_bf16(jnp.dot(query_gradient, up_projection_broad.T, precision=highest_precision))
    hidden_state_factor = to_bf16(jnp.dot(hidden_state, output_down, preferred_element_type=jnp.float32))
    contraction_rows = (((0,), (0,)), ((), ()))
    query_down_gradient = adapter_scale * lax.dot_general(activations, query_lowrank_factor, contraction_rows, preferred_element_type=jnp.float32)
    query_up_gradient = adapter_scale * jnp.dot(input_lowrank_factor.T, query_gradient, precision=highest_precision)
    output_down_gradient = adapter_scale * jnp.dot(hidden_state.astype(jnp.float32).T, gradient_lowrank_factor, precision=highest_precision)
    output_up_gradient = adapter_scale * lax.dot_general(hidden_state_factor, output_gradient, contraction_rows, preferred_element_type=jnp.float32)
    return (query_down_gradient, query_up_gradient, output_down_gradient, output_up_gradient)
```

```python
import functools
import math

import jax
import jax.numpy as jnp
from jax import lax
from jax.experimental import pallas as pl
from jax.experimental.pallas import tpu as pltpu
from jax.sharding import PartitionSpec as P

HD = 128
HEADS = 64
KVH = 4

SCALE = 0.5
BF = jnp.bfloat16
F32 = jnp.float32


def mm(left, right, a, b):
    return lax.dot_general(
        left, right, (((a,), (b,)), ((), ())), preferred_element_type=F32
    )


def kernel(
    n_row,
    n_col,
    lengths_hbm,
    forget_hbm,
    x_hbm,
    cot_hbm,
    wq_hbm,
    wk_hbm,
    wv_hbm,
    wo_hbm,
    qd_hbm,
    up_hbm,
    od_hbm,
    ou_hbm,
    dq_ref,
    pieces_ref,
    du_ref,
    x,
    cot,
    wq,
    kvw,
    wo,
    qd,
    up,
    od,
    ou,
    red,
    part_all,
    qt,
    ht,
    kv_send,
    kv_recv,
    kv_all,
    ends_all,
    bd,
    sel,
    same_all,
    s_send,
    s_recv,
    pg_send,
    pg_recv,
    low_send,
    low_recv,
    fac_send,
    fac_recv,
    fac_all,
    m_all,
    fac_cat,
    lengths_ref,
    forget_ref,
    load_sem,
    wq_sem,
    wo_sem,
    kv_sem,
    mate_sem,
    ends_sem,
    s_sem,
    low_ss,
    low_rs,
    part_sem,
    pg_ss,
    pg_rs,
    fac_ss,
    fac_rs,
    all_ss,
    all_rs,
    m_ss,
    m_rs,
):
    me = lax.axis_index("row")
    mc = lax.axis_index("col")
    n_chunk, depth, width = wq.shape
    n_quad = s_send.shape[1]
    rank = qd.shape[0]
    tokens = x.shape[0]
    blk = tokens // n_row
    cols = n_chunk * width
    heads = cols // HD
    pack = blk // 2
    inverse = 1.0 / math.sqrt(HD)
    group = lax.div(mc * heads, HEADS // KVH)
    group_cols = pl.ds(pl.multiple_of(group * HD, HD), HD)
    role = lax.rem(mc, 2)
    mate = mc + 1 - 2 * role
    others = pl.ds(1, n_row - 1)

    def row_peer(d):
        return lax.rem(me + d, n_row)

    def col_peer(d):
        return lax.rem(mc + d, n_col)

    def alone(body):
        pl.when(mc >= 0)(body)

    def settle(ref, sem):
        pltpu.make_async_copy(ref, ref, sem).wait()

    def load_wq(c):
        return pltpu.make_async_copy(
            wq_hbm.at[:, pl.ds(c * width, width)], wq.at[c], wq_sem.at[c]
        )

    units = [(0, min(2 * width, cols))] + [(first, width) for first in range(2 * width, cols, width)]

    def load_wo(i):
        span = pl.ds(*units[i])
        return pltpu.make_async_copy(wo_hbm.at[span], wo.at[span], wo_sem.at[i])

    load_x = pltpu.make_async_copy(x_hbm, x, load_sem.at[0])
    load_qd = pltpu.make_async_copy(qd_hbm, qd, load_sem.at[1])
    load_k = pltpu.make_async_copy(wk_hbm.at[:, group_cols], kvw.at[:, pl.ds(0, HD)], load_sem.at[2])
    load_v = pltpu.make_async_copy(wv_hbm.at[:, group_cols], kvw.at[:, pl.ds(0, HD)], load_sem.at[2])
    load_cot = pltpu.make_async_copy(cot_hbm, cot, load_sem.at[3])
    load_ou = pltpu.make_async_copy(ou_hbm, ou, load_sem.at[4])
    load_len = pltpu.make_async_copy(lengths_hbm, lengths_ref, load_sem.at[5])
    load_forget = pltpu.make_async_copy(forget_hbm, forget_ref, load_sem.at[6])
    load_up = pltpu.make_async_copy(up_hbm, up, load_sem.at[7])
    load_od = pltpu.make_async_copy(od_hbm, od, load_sem.at[8])
    load_len.start()
    load_qd.start()
    load_x.start()

    @pl.when(role == 0)
    def _():
        load_k.start()

    @pl.when(role == 1)
    def _():
        load_v.start()

    load_wq(0).start()
    load_up.start()

    barrier = pltpu.get_barrier_semaphore()

    def greet(where):
        pl.semaphore_signal(barrier, inc=1, device_id=where, device_id_type=pl.DeviceIdType.MESH)

    for d in range(1, n_row):
        greet({"row": row_peer(d)})
    for d in range(1, n_col):
        greet({"col": col_peer(d)})

    def remote(src, dst, send, recv, where):
        return pltpu.make_async_remote_copy(
            src_ref=src,
            dst_ref=dst,
            send_sem=send,
            recv_sem=recv,
            device_id=where,
            device_id_type=pl.DeviceIdType.MESH,
        )

    def ends_copy(d):
        return remote(ends_all.at[me], ends_all.at[me], ends_sem.at[0], ends_sem.at[1], {"row": row_peer(d)})

    def kv_copy(d):
        return remote(kv_send, kv_recv.at[d], kv_sem.at[0], kv_sem.at[1], {"row": row_peer(d)})

    mate_copy = remote(kv_all.at[role], kv_all.at[role], mate_sem.at[0], mate_sem.at[1], {"col": mate})

    def s_copy(d):
        p = row_peer(d)
        return remote(s_send.at[p], s_recv.at[d], s_sem.at[0], s_sem.at[1], {"row": p})

    def pg_copy(q, d):
        p = row_peer(d)
        return remote(pg_send.at[q, p], pg_recv.at[q, d], pg_ss.at[q], pg_rs.at[q], {"row": p})

    def part_copy(d):
        return remote(part_all.at[mc], part_all.at[mc], part_sem.at[0], part_sem.at[1], {"col": col_peer(d)})

    def low_copy(j, d):
        p = row_peer(d)
        return remote(low_send.at[j, p], low_recv.at[j, d], low_ss.at[j], low_rs.at[j], {"row": p})

    def fac_copy(j, d):
        return remote(fac_send.at[j], fac_recv.at[j, d], fac_ss.at[j], fac_rs.at[j], {"col": col_peer(d)})

    def all_copy(j, d):
        return remote(fac_all.at[j, me], fac_all.at[j, me], all_ss.at[j], all_rs.at[j], {"row": row_peer(d)})

    def m_copy(j, d):
        return remote(m_all.at[j, me], m_all.at[j, me], m_ss.at[j], m_rs.at[j], {"row": row_peer(d)})

    quarter = blk // 4

    def pack_rows(block):
        return jnp.concatenate([block[i * quarter : (i + 1) * quarter] for i in range(4)], axis=1)

    def unpack_rows(block):
        return jnp.concatenate([block[:, i * rank : (i + 1) * rank] for i in range(4)], axis=0)

    def send_low(j, partial):
        for r in range(n_row):
            low_send[j, r] = pack_rows(partial[r * blk : (r + 1) * blk])
        for d in range(1, n_row):
            low_copy(j, d).start()

    def sum_low(j):
        settle(low_recv.at[j, others], low_rs.at[j])
        low = low_send[j, me].astype(F32)
        for d in range(1, n_row):
            low = low + low_recv[j, d].astype(F32)
        return unpack_rows(low)

    def send_factor(j, factor):
        fac_send[j] = pack_rows(factor).astype(BF)
        for d in range(1, n_col):
            fac_copy(j, d).start()

    def spread_factor(j):
        settle(fac_recv.at[j, pl.ds(1, n_col - 1)], fac_rs.at[j])
        total = fac_send[j].astype(F32)
        for d in range(1, n_col):
            total = total + fac_recv[j, d].astype(F32)
        fac_all[j, me] = total.astype(BF)
        for d in range(1, n_row):
            all_copy(j, d).start()

    def factor_everywhere(j):
        settle(fac_all.at[j, others], all_rs.at[j])
        blocks = []
        for r in range(n_row):
            blocks.append(unpack_rows(fac_all[j, r].astype(F32)))
        return blocks

    def send_moment(j, low, cat):
        moment = (SCALE * mm(low, cat, 0, 0)).astype(BF)
        for c in range(n_chunk):
            m_all[j, me, c * rank : (c + 1) * rank, :] = moment[:, c * 2 * blk : (c + 1) * 2 * blk]
        for d in range(1, n_row):
            m_copy(j, d).start()

    def finish_moment(j):
        settle(m_all.at[j, others], m_rs.at[j])

        @alone
        def _():
            total = mm(m_all[j, 0], bd[j, 0], 1, 0)
            for r in range(1, n_row):
                total = total + mm(m_all[j, r], bd[j, r], 1, 0)
            for c in range(n_chunk):
                pieces_ref[j * rank : (j + 1) * rank, c * width : (c + 1) * width] = total[
                    c * rank : (c + 1) * rank
                ]

    lane = lax.broadcasted_iota(jnp.int32, (blk, 2 * blk), 1)
    token_f = lax.broadcasted_iota(jnp.int32, (blk, 2 * blk), 0).astype(F32)
    key_f = lax.rem(lane, blk).astype(F32)
    slot_f = lax.rem(lane, pack).astype(F32)
    head_of = lax.div(lane, pack)

    def ends_of(r):
        return [ends_all[r, i : i + 1, :] for i in range(lengths_ref.shape[1])]

    def same_document(r):
        query_seg = jnp.zeros((blk, 2 * blk), F32)
        key_seg = jnp.zeros((blk, 2 * blk), F32)
        for end in ends_of(r):
            query_seg = query_seg + jnp.where(token_f >= end, 1.0, 0.0)
            key_seg = key_seg + jnp.where(key_f >= end, 1.0, 0.0)
        return query_seg == key_seg

    def place_in_document(r):
        start = jnp.zeros((blk, 2 * blk), F32)
        for end in ends_of(r):
            start = jnp.where(token_f >= end, end, start)
        return token_f - start

    def fold(r, parts):
        kept = [part.astype(BF) * same_all[r] for part in parts]
        rows = [jnp.concatenate(kept[i : i + 2], axis=1) for i in range(0, len(kept), 2)]
        rows = jnp.concatenate(rows, axis=0)
        return mm(rows, sel[r, 0 : rows.shape[1]], 1, 0)

    def split_rows(part):
        return [part[i * blk : (i + 1) * blk] for i in range(part.shape[0] // blk)]

    load_len.wait()
    rows8 = lax.broadcasted_iota(jnp.int32, (8, 2 * blk), 0)
    tile = jnp.zeros((8, 2 * blk), jnp.int32)
    end = 0
    for i in range(lengths_ref.shape[1]):
        end = end + lengths_ref[0, i]
        tile = jnp.where(rows8 == i, end, tile)
    ends_all[me] = tile.astype(F32)
    load_qd.wait()
    kvw[:, HD:] = jnp.concatenate([qd[...].T, jnp.zeros((depth, HD - rank), BF)], axis=1)
    load_x.wait()
    if n_chunk > 1:
        load_wq(1).start()
    load_k.wait()
    if n_chunk > 2:
        load_wq(2).start()

    @alone
    def _():
        both = mm(x[...], kvw[...], 1, 0).astype(BF)
        kv_send[...] = both[:, 0:HD]
        red[...] = both[:, HD : HD + rank]

    pl.semaphore_wait(barrier, n_row + n_col - 2)
    for d in range(1, n_row):
        ends_copy(d).start()
    for d in range(1, n_row):
        kv_copy(d).start()
    send_low(0, red[...])

    def forward(c):
        load_wq(c).wait()

        @alone
        def _():
            term = mm(x[...], wq[c], 1, 0)
            qt[:, c] = term.astype(BF).reshape(n_row, blk, width)

    def low_part():
        load_cot.wait()
        load_ou.wait()

        @alone
        def _():
            own = tokens // n_col
            first = pl.multiple_of(mc * own, own)
            part = mm(cot[pl.ds(first, own), :], ou[...], 1, 1)
            part_all[mc] = jnp.concatenate([part, jnp.zeros((own, HD - rank), F32)], axis=1).astype(BF)

        for d in range(1, n_col):
            part_copy(d).start()

    for c in range(n_chunk):
        forward(c)
        if c == 0:
            load_cot.start()
            load_ou.start()
            for i in range(3, n_chunk):
                load_wq(i).start()
            load_wo(0).start()
        if c == min(1, n_chunk - 1):
            for i in range(1, len(units)):
                load_wo(i).start()
            load_od.start()
            load_forget.start()
        if c == min(2, n_chunk - 1):
            low_part()

    settle(ends_all.at[others], ends_sem.at[1])
    for r in range(n_row):
        same_all[r] = jnp.where(same_document(r), 1.0, 0.0).astype(BF)
        hit = place_in_document(r) == slot_f
        for h in range(4):
            sel[r, h * blk : (h + 1) * blk, :] = jnp.where(hit & (head_of == h), 1.0, 0.0).astype(BF)

    def backward(i):
        load_wo(i).wait()

        @alone
        def _():
            first, size = units[i]
            term = mm(cot[...], wo[pl.ds(first, size)], 1, 1).astype(BF)
            for k in range(size // width):
                ht[:, first // width + k] = term[:, k * width : (k + 1) * width].reshape(n_row, blk, width)

    def send_prob(q):

        @alone
        def _():
            count = min(2, n_chunk - 2 * q)
            wide = [
                mm(ht[r, 2 * q : 2 * q + count].reshape(count * blk, width), bd[1, r], 1, 1)
                for r in range(n_row)
            ]
            for r in range(n_row):
                pg_send[q, r] = fold(r, split_rows(wide[r])).astype(BF)

        for d in range(1, n_row):
            pg_copy(q, d).start()

    backward(0)
    settle(kv_recv.at[others], kv_sem.at[1])
    total = kv_send[...].astype(F32)
    for d in range(1, n_row):
        total = total + kv_recv[d].astype(F32)
    kv_all[role] = total.astype(BF)
    mate_copy.start()
    if len(units) > 1:
        backward(1)
    settle(kv_all.at[1 - role], mate_sem.at[1])
    empty = jnp.zeros((blk, HD), BF)
    for j in range(2):
        for r in range(n_row):
            block = kv_all[j, r * blk : (r + 1) * blk]
            bd[j, r] = jnp.concatenate(
                [jnp.concatenate([block, empty], axis=1), jnp.concatenate([empty, block], axis=1)], axis=0
            )

    @alone
    def _():
        wide = [mm(qt[r].reshape(n_chunk * blk, width), bd[0, r], 1, 1) for r in range(n_row)]
        for r in range(n_row):
            s_send[r] = fold(r, split_rows(wide[r])).astype(BF).reshape(n_quad, blk, 2 * blk)

    for d in range(1, n_row):
        s_copy(d).start()
    settle(part_all.at[pl.ds(1, n_col - 1)], part_sem.at[1])
    send_low(1, part_all[...].reshape(tokens, HD)[:, 0:rank])
    send_prob(0)
    for i in range(2, len(units)):
        backward(i)
    for q in range(1, n_quad):
        send_prob(q)

    def sign_of(first):
        lane = lax.broadcasted_iota(jnp.int32, (blk, tokens), 1)
        sub = lax.broadcasted_iota(jnp.int32, (blk, tokens), 0)
        picked = jnp.where(lane == sub + first, forget_ref[...], 0)
        return (1 - 2 * jnp.sum(picked, axis=1, keepdims=True)).astype(F32)

    load_forget.wait()
    load_up.wait()
    load_od.wait()
    sign = sign_of(me * blk)
    ku = jnp.concatenate(
        [mm(bd[0, me], up[:, c * width : (c + 1) * width], 1, 1) for c in range(n_chunk)], axis=0
    ).astype(BF)
    vo = jnp.concatenate(
        [mm(bd[1, me], od[:, c * width : (c + 1) * width], 1, 1) for c in range(n_chunk)], axis=0
    ).astype(BF)
    same = same_document(me)
    allowed = slot_f <= place_in_document(me)
    wide = lax.broadcasted_iota(jnp.int32, (4 * blk, 2 * blk), 0)
    narrow = lax.broadcasted_iota(jnp.int32, (4 * blk, 2 * blk), 1)
    ones = jnp.where(lax.div(lax.rem(wide, 2 * blk), pack) == lax.div(narrow, pack), 1.0, 0.0).astype(BF)

    def head_sum(values):
        high = values.astype(BF)
        low = (values - high.astype(F32)).astype(BF)
        return mm(jnp.concatenate([high, low], axis=1), ones, 1, 0)

    def stack(blocks):
        return jnp.concatenate(blocks, axis=0)

    def unfold(values):
        open_ = mm(values.astype(BF), sel[me], 1, 1)
        keep = jnp.concatenate([same, same], axis=1)
        parts = [jnp.where(keep, open_[q * blk : (q + 1) * blk], 0.0) for q in range(n_quad)]
        return jnp.concatenate(parts, axis=1)[:, 0 : n_chunk * 2 * blk].astype(BF)

    def spread_low(low, narrow):
        wide = SCALE * mm(low, narrow, 1, 1)
        return fold(me, [wide[:, c * 2 * blk : (c + 1) * 2 * blk] for c in range(n_chunk)])

    in_low = sum_low(0).astype(BF)
    score_low = spread_low(in_low, ku)

    settle(s_recv.at[others], s_sem.at[1])
    total = s_send[me].astype(F32)
    for d in range(1, n_row):
        total = total + s_recv[d].astype(F32)
    total = total.reshape(n_quad * blk, 2 * blk) + score_low
    numer = jnp.where(stack([allowed] * n_quad), jnp.exp(total * inverse), 0.0)
    soft = numer / head_sum(numer)
    cat = unfold(soft)
    send_factor(1, mm(cat, vo, 1, 0))
    grad_low = (sum_low(1) * sign).astype(BF)
    prob_low = spread_low(grad_low, vo)
    send_moment(1, grad_low, cat)

    grads = []
    for q in range(n_quad):
        settle(pg_recv.at[q, others], pg_rs.at[q])
        total = pg_send[q, me].astype(F32)
        for d in range(1, n_row):
            total = total + pg_recv[q, d].astype(F32)
        grads.append(total * sign)
    total = stack(grads) + prob_low
    total = soft * (total - head_sum(total * soft)) * inverse
    cat = unfold(total)
    send_factor(0, mm(cat, ku, 1, 0))
    send_moment(0, in_low, cat)
    signs = [sign_of(r * blk) for r in range(n_row)]
    spread_factor(1)
    spread_factor(0)
    finish_moment(1)
    blocks = [(b * s).astype(BF) for b, s in zip(factor_everywhere(1), signs)]
    fac_cat[0] = jnp.concatenate(blocks, axis=0)

    @alone
    def _():
        du_ref[...] = SCALE * mm(fac_cat[0], cot[...], 0, 0)

    finish_moment(0)
    blocks = [b.astype(BF) for b in factor_everywhere(0)]
    fac_cat[1] = jnp.concatenate(blocks, axis=0)

    @alone
    def _():
        dq_ref[...] = SCALE * mm(fac_cat[1], x[...], 0, 0)

    settle(kv_recv.at[others], kv_sem.at[0])
    settle(kv_all.at[role], mate_sem.at[0])
    settle(ends_all.at[others], ends_sem.at[0])
    settle(s_recv.at[others], s_sem.at[0])
    settle(part_all.at[pl.ds(1, n_col - 1)], part_sem.at[0])
    for q in range(n_quad):
        settle(pg_recv.at[q, others], pg_ss.at[q])
    for j in range(2):
        settle(low_recv.at[j, others], low_ss.at[j])
        settle(fac_recv.at[j, pl.ds(1, n_col - 1)], fac_ss.at[j])
        settle(fac_all.at[j, others], all_ss.at[j])
        settle(m_all.at[j, others], m_ss.at[j])


def writer(dq, pieces, du, o_qd, o_up, o_od, o_ou, sem):
    rank = dq.shape[0]
    moves = [
        pltpu.make_async_copy(dq, o_qd, sem.at[0]),
        pltpu.make_async_copy(du, o_ou, sem.at[1]),
        pltpu.make_async_copy(pieces.at[pl.ds(0, rank)], o_up, sem.at[2]),
        pltpu.make_async_copy(pieces.at[pl.ds(rank, rank)], o_od, sem.at[3]),
    ]
    for move in moves:
        move.start()
    for move in moves:
        move.wait()


def local(
    activations,
    cotangent,
    forget,
    lengths,
    query_weight,
    key_weight,
    value_weight,
    output_projection_weight,
    query_down,
    query_up,
    output_down,
    output_up,
):
    n_row, n_col = lax.axis_size("row"), lax.axis_size("col")
    tokens, depth = activations.shape
    cols = query_weight.shape[1]
    rank = query_down.shape[1]
    blk = tokens // n_row
    width = 2 * HD
    n_chunk = cols // width
    n_quad = (n_chunk + 1) // 2
    hbm = pl.BlockSpec(memory_space=pltpu.HBM)
    vmem = pl.BlockSpec(memory_space=pltpu.VMEM)
    dma = pltpu.SemaphoreType.DMA
    dq, pieces, du = pl.pallas_call(
        functools.partial(kernel, n_row, n_col),
        out_shape=(
            jax.ShapeDtypeStruct((rank, depth), F32),
            jax.ShapeDtypeStruct((2 * rank, cols), F32),
            jax.ShapeDtypeStruct((rank, depth), F32),
        ),
        in_specs=[hbm] * 12,
        out_specs=(vmem, vmem, vmem),
        scratch_shapes=[
            pltpu.VMEM((tokens, depth), BF),
            pltpu.VMEM((tokens, depth), BF),
            pltpu.VMEM((n_chunk, depth, width), BF),
            pltpu.VMEM((depth, 2 * HD), BF),
            pltpu.VMEM((cols, depth), BF),
            pltpu.VMEM((rank, depth), BF),
            pltpu.VMEM((rank, cols), BF),
            pltpu.VMEM((rank, cols), BF),
            pltpu.VMEM((rank, depth), BF),
            pltpu.VMEM((tokens, rank), BF),
            pltpu.VMEM((n_col, tokens // n_col, HD), BF),
            pltpu.VMEM((n_row, n_chunk, blk, width), BF),
            pltpu.VMEM((n_row, n_chunk, blk, width), BF),
            pltpu.VMEM((tokens, HD), BF),
            pltpu.VMEM((n_row, tokens, HD), BF),
            pltpu.VMEM((2, tokens, HD), BF),
            pltpu.VMEM((n_row, 8, 2 * blk), F32),
            pltpu.VMEM((2, n_row, 2 * blk, 2 * HD), BF),
            pltpu.VMEM((n_row, 4 * blk, 2 * blk), BF),
            pltpu.VMEM((n_row, blk, 2 * blk), BF),
            pltpu.VMEM((n_row, n_quad, blk, 2 * blk), BF),
            pltpu.VMEM((n_row, n_quad, blk, 2 * blk), BF),
            pltpu.VMEM((n_quad, n_row, blk, 2 * blk), BF),
            pltpu.VMEM((n_quad, n_row, blk, 2 * blk), BF),
            pltpu.VMEM((2, n_row, blk // 4, 4 * rank), BF),
            pltpu.VMEM((2, n_row, blk // 4, 4 * rank), BF),
            pltpu.VMEM((2, blk // 4, 4 * rank), BF),
            pltpu.VMEM((2, n_col, blk // 4, 4 * rank), BF),
            pltpu.VMEM((2, n_row, blk // 4, 4 * rank), BF),
            pltpu.VMEM((2, n_row, n_chunk * rank, 2 * blk), BF),
            pltpu.VMEM((2, tokens, rank), BF),
            pltpu.SMEM(lengths.shape, jnp.int32),
            pltpu.VMEM((1, tokens), jnp.int32),
            dma((9,)),
            dma((n_chunk,)),
            dma((n_chunk,)),
            dma((2,)),
            dma((2,)),
            dma((2,)),
            dma((2,)),
            dma((2,)),
            dma((2,)),
            dma((2,)),
            dma((n_quad,)),
            dma((n_quad,)),
            dma((2,)),
            dma((2,)),
            dma((2,)),
            dma((2,)),
            dma((2,)),
            dma((2,)),
        ],
        compiler_params=pltpu.CompilerParams(
            collective_id=0, has_side_effects=True, vmem_limit_bytes=50 << 20
        ),
        name="unlearn_step",
    )(
        *(
            pltpu.with_memory_space_constraint(operand, pltpu.HBM)
            for operand in (
                lengths,
                forget.reshape(1, tokens),
                activations,
                cotangent,
                query_weight,
                key_weight,
                value_weight,
                output_projection_weight,
                query_down.T,
                query_up,
                output_down.T,
                output_up,
            )
        )
    )
    down_grad, up_grad, out_down_grad, out_up_grad = pl.pallas_call(
        writer,
        out_shape=(
            jax.ShapeDtypeStruct((rank, depth), F32),
            jax.ShapeDtypeStruct((rank, cols), F32),
            jax.ShapeDtypeStruct((rank, cols), F32),
            jax.ShapeDtypeStruct((rank, depth), F32),
        ),
        in_specs=[pl.BlockSpec(memory_space=pl.ANY)] * 3,
        out_specs=(hbm,) * 4,
        scratch_shapes=[dma((4,))],
        compiler_params=pltpu.CompilerParams(vmem_limit_bytes=1 << 20),
        name="write_outputs",
    )(dq, pieces, du)
    return down_grad.T, up_grad, out_down_grad.T, out_up_grad


def solution(mesh):
    placed = (
        P(None, "row"),
        P(None, "row"),
        P(),
        P("row", None),
        P("row", "col"),
        P("row", None),
        P("row", None),
        P("col", "row"),
        P("row", None),
        P(None, "col"),
        P("col", None),
        P(None, "row"),
    )
    return jax.shard_map(
        local,
        mesh=mesh,
        in_specs=placed,
        out_specs=(P("row", None), P(None, "col"), P("col", None), P(None, "row")),
        check_vma=False,
    )
```

```python
import functools
import math

import jax
import jax.numpy as jnp
from jax import lax
from jax.experimental import pallas as pl
from jax.experimental.pallas import tpu as pltpu
from jax.sharding import PartitionSpec as P

HD = 128
HEADS = 64
KVH = 4

SCALE = 0.5
DIRECT = 64
BF = jnp.bfloat16
F32 = jnp.float32


def mm(left, right, a, b):
    return lax.dot_general(
        left, right, (((a,), (b,)), ((), ())), preferred_element_type=F32
    )


def kernel(
    n_row,
    n_col,
    lengths_hbm,
    forget_hbm,
    x_hbm,
    cot_hbm,
    wq_hbm,
    wk_hbm,
    wv_hbm,
    wo_hbm,
    qd_hbm,
    up_hbm,
    od_hbm,
    ou_hbm,
    dq_ref,
    pieces_ref,
    du_ref,
    x,
    cot,
    wq,
    kvw,
    wo,
    qd,
    up,
    od,
    ou,
    red,
    part_all,
    qt,
    ht,
    kv_send,
    kv_recv,
    kv_all,
    ends_all,
    bd,
    sel,
    same_all,
    s_send,
    s_recv,
    pg_send,
    pg_recv,
    low_send,
    low_recv,
    fac_send,
    fac_recv,
    fac_all,
    fac_every,
    m_all,
    fac_cat,
    lengths_ref,
    forget_ref,
    load_sem,
    wq_sem,
    wo_sem,
    kv_sem,
    mate_sem,
    ends_sem,
    s_sem,
    low_ss,
    low_rs,
    part_sem,
    pg_ss,
    pg_rs,
    fac_ss,
    fac_rs,
    all_ss,
    all_rs,
    m_ss,
    m_rs,
    every_ss,
    every_rs,
):
    me = lax.axis_index("row")
    mc = lax.axis_index("col")
    n_chunk, depth, width = wq.shape
    n_quad = s_send.shape[1]
    rank = qd.shape[0]
    tokens = x.shape[0]
    blk = tokens // n_row
    cols = n_chunk * width
    heads = cols // HD
    pack = blk // 2
    inverse = 1.0 / math.sqrt(HD)
    group = lax.div(mc * heads, HEADS // KVH)
    group_cols = pl.ds(pl.multiple_of(group * HD, HD), HD)
    role = lax.rem(mc, 2)
    mate = mc + 1 - 2 * role
    others = pl.ds(1, n_row - 1)

    def row_peer(d):
        return lax.rem(me + d, n_row)

    def col_peer(d):
        return lax.rem(mc + d, n_col)

    def alone(body):
        pl.when(mc >= 0)(body)

    def settle(ref, sem):
        pltpu.make_async_copy(ref, ref, sem).wait()

    def load_wq(c):
        return pltpu.make_async_copy(
            wq_hbm.at[:, pl.ds(c * width, width)], wq.at[c], wq_sem.at[c]
        )

    units = [(0, min(2 * width, cols))] + [(first, width) for first in range(2 * width, cols, width)]

    def load_wo(i):
        span = pl.ds(*units[i])
        return pltpu.make_async_copy(wo_hbm.at[span], wo.at[span], wo_sem.at[i])

    load_x = pltpu.make_async_copy(x_hbm, x, load_sem.at[0])
    load_qd = pltpu.make_async_copy(qd_hbm, qd, load_sem.at[1])
    load_k = pltpu.make_async_copy(wk_hbm.at[:, group_cols], kvw.at[:, pl.ds(0, HD)], load_sem.at[2])
    load_v = pltpu.make_async_copy(wv_hbm.at[:, group_cols], kvw.at[:, pl.ds(0, HD)], load_sem.at[2])
    load_cot = pltpu.make_async_copy(cot_hbm, cot, load_sem.at[3])
    load_ou = pltpu.make_async_copy(ou_hbm, ou, load_sem.at[4])
    load_len = pltpu.make_async_copy(lengths_hbm, lengths_ref, load_sem.at[5])
    load_forget = pltpu.make_async_copy(forget_hbm, forget_ref, load_sem.at[6])
    load_up = pltpu.make_async_copy(up_hbm, up, load_sem.at[7])
    load_od = pltpu.make_async_copy(od_hbm, od, load_sem.at[8])
    load_len.start()
    load_qd.start()
    load_x.start()

    @pl.when(role == 0)
    def _():
        load_k.start()

    @pl.when(role == 1)
    def _():
        load_v.start()

    load_wq(0).start()
    load_up.start()

    barrier = pltpu.get_barrier_semaphore()

    def greet(where):
        pl.semaphore_signal(barrier, inc=1, device_id=where, device_id_type=pl.DeviceIdType.MESH)

    for d in range(1, n_row):
        greet({"row": row_peer(d)})
    for d in range(1, n_col):
        greet({"col": col_peer(d)})

    def remote(src, dst, send, recv, where):
        return pltpu.make_async_remote_copy(
            src_ref=src,
            dst_ref=dst,
            send_sem=send,
            recv_sem=recv,
            device_id=where,
            device_id_type=pl.DeviceIdType.MESH,
        )

    def ends_copy(d):
        return remote(ends_all.at[me], ends_all.at[me], ends_sem.at[0], ends_sem.at[1], {"row": row_peer(d)})

    def kv_copy(d):
        return remote(kv_send, kv_recv.at[d], kv_sem.at[0], kv_sem.at[1], {"row": row_peer(d)})

    mate_copy = remote(kv_all.at[role], kv_all.at[role], mate_sem.at[0], mate_sem.at[1], {"col": mate})

    def s_copy(d):
        p = row_peer(d)
        return remote(s_send.at[p], s_recv.at[d], s_sem.at[0], s_sem.at[1], {"row": p})

    def pg_copy(q, d):
        p = row_peer(d)
        return remote(pg_send.at[q, p], pg_recv.at[q, d], pg_ss.at[q], pg_rs.at[q], {"row": p})

    def part_copy(d):
        return remote(part_all.at[mc], part_all.at[mc], part_sem.at[0], part_sem.at[1], {"col": col_peer(d)})

    def low_copy(j, d):
        p = row_peer(d)
        return remote(low_send.at[j, p], low_recv.at[j, d], low_ss.at[j], low_rs.at[j], {"row": p})

    def fac_copy(j, d):
        return remote(fac_send.at[j], fac_recv.at[j, d], fac_ss.at[j], fac_rs.at[j], {"col": col_peer(d)})

    def all_copy(j, d):
        return remote(fac_all.at[j, me], fac_all.at[j, me], all_ss.at[j], all_rs.at[j], {"row": row_peer(d)})

    def m_copy(j, d):
        return remote(m_all.at[j, me], m_all.at[j, me], m_ss.at[j], m_rs.at[j], {"row": row_peer(d)})

    quarter = blk // 4

    def pack_rows(block):
        return jnp.concatenate([block[i * quarter : (i + 1) * quarter] for i in range(4)], axis=1)

    def unpack_rows(block):
        return jnp.concatenate([block[:, i * rank : (i + 1) * rank] for i in range(4)], axis=0)

    def send_low(j, partial):
        for r in range(n_row):
            low_send[j, r] = pack_rows(partial[r * blk : (r + 1) * blk])
        for d in range(1, n_row):
            low_copy(j, d).start()

    def sum_low(j):
        settle(low_recv.at[j, others], low_rs.at[j])
        low = low_send[j, me].astype(F32)
        for d in range(1, n_row):
            low = low + low_recv[j, d].astype(F32)
        return unpack_rows(low)

    direct = n_row * n_col <= DIRECT
    pairs = n_col // 2
    place = me * pairs + lax.div(mc, 2)

    def fac_swap(j):
        return remote(fac_send.at[j], fac_recv.at[j, 1], fac_ss.at[j], fac_rs.at[j], {"col": mate})

    def every_copy(j, a, b):
        return remote(
            fac_every.at[j, place],
            fac_every.at[j, place],
            every_ss.at[j],
            every_rs.at[j],
            {"row": row_peer(a), "col": col_peer(2 * b)},
        )

    def send_factor(j, factor):
        fac_send[j] = pack_rows(factor).astype(BF)
        if direct:
            fac_swap(j).start()
            return
        for d in range(1, n_col):
            fac_copy(j, d).start()

    def spread_factor(j):
        if direct:
            settle(fac_recv.at[j, pl.ds(1, 1)], fac_rs.at[j])
            fac_every[j, place] = (fac_send[j].astype(F32) + fac_recv[j, 1].astype(F32)).astype(BF)
            for b in [*range(1, pairs), 0]:
                for a in range(n_row):
                    if a + b > 0:
                        every_copy(j, a, b).start()
            return
        settle(fac_recv.at[j, pl.ds(1, n_col - 1)], fac_rs.at[j])
        total = fac_send[j].astype(F32)
        for d in range(1, n_col):
            total = total + fac_recv[j, d].astype(F32)
        fac_all[j, me] = total.astype(BF)
        for d in range(1, n_row):
            all_copy(j, d).start()

    def factor_everywhere(j):
        if direct:
            settle(fac_every.at[j, pl.ds(1, n_row * pairs - 1)], every_rs.at[j])
            blocks = []
            for r in range(n_row):
                total = fac_every[j, r * pairs].astype(F32)
                for c in range(1, pairs):
                    total = total + fac_every[j, r * pairs + c].astype(F32)
                blocks.append(unpack_rows(total))
            return blocks
        settle(fac_all.at[j, others], all_rs.at[j])
        blocks = []
        for r in range(n_row):
            blocks.append(unpack_rows(fac_all[j, r].astype(F32)))
        return blocks

    def send_moment(j, low, cat):
        moment = (SCALE * mm(low, cat, 0, 0)).astype(BF)
        for c in range(n_chunk):
            m_all[j, me, c * rank : (c + 1) * rank, :] = moment[:, c * 2 * blk : (c + 1) * 2 * blk]
        for d in range(1, n_row):
            m_copy(j, d).start()

    def finish_moment(j):
        settle(m_all.at[j, others], m_rs.at[j])

        @alone
        def _():
            total = mm(m_all[j, 0], bd[j, 0], 1, 0)
            for r in range(1, n_row):
                total = total + mm(m_all[j, r], bd[j, r], 1, 0)
            for c in range(n_chunk):
                pieces_ref[j * rank : (j + 1) * rank, c * width : (c + 1) * width] = total[
                    c * rank : (c + 1) * rank
                ]

    lane = lax.broadcasted_iota(jnp.int32, (blk, 2 * blk), 1)
    token_f = lax.broadcasted_iota(jnp.int32, (blk, 2 * blk), 0).astype(F32)
    key_f = lax.rem(lane, blk).astype(F32)
    slot_f = lax.rem(lane, pack).astype(F32)
    head_of = lax.div(lane, pack)

    def ends_of(r):
        return [ends_all[r, i : i + 1, :] for i in range(lengths_ref.shape[1])]

    def same_document(r):
        query_seg = jnp.zeros((blk, 2 * blk), F32)
        key_seg = jnp.zeros((blk, 2 * blk), F32)
        for end in ends_of(r):
            query_seg = query_seg + jnp.where(token_f >= end, 1.0, 0.0)
            key_seg = key_seg + jnp.where(key_f >= end, 1.0, 0.0)
        return query_seg == key_seg

    def place_in_document(r):
        start = jnp.zeros((blk, 2 * blk), F32)
        for end in ends_of(r):
            start = jnp.where(token_f >= end, end, start)
        return token_f - start

    def fold(r, parts):
        kept = [part.astype(BF) * same_all[r] for part in parts]
        rows = [jnp.concatenate(kept[i : i + 2], axis=1) for i in range(0, len(kept), 2)]
        rows = jnp.concatenate(rows, axis=0)
        return mm(rows, sel[r, 0 : rows.shape[1]], 1, 0)

    def split_rows(part):
        return [part[i * blk : (i + 1) * blk] for i in range(part.shape[0] // blk)]

    load_len.wait()
    rows8 = lax.broadcasted_iota(jnp.int32, (8, 2 * blk), 0)
    tile = jnp.zeros((8, 2 * blk), jnp.int32)
    end = 0
    for i in range(lengths_ref.shape[1]):
        end = end + lengths_ref[0, i]
        tile = jnp.where(rows8 == i, end, tile)
    ends_all[me] = tile.astype(F32)
    load_qd.wait()
    kvw[:, HD:] = jnp.concatenate([qd[...].T, jnp.zeros((depth, HD - rank), BF)], axis=1)
    load_x.wait()
    if n_chunk > 1:
        load_wq(1).start()
    load_k.wait()
    if n_chunk > 2:
        load_wq(2).start()

    @alone
    def _():
        both = mm(x[...], kvw[...], 1, 0).astype(BF)
        kv_send[...] = both[:, 0:HD]
        red[...] = both[:, HD : HD + rank]

    load_cot.start()
    load_ou.start()
    pl.semaphore_wait(barrier, n_row + n_col - 2)
    for d in range(1, n_row):
        ends_copy(d).start()
    for d in range(1, n_row):
        kv_copy(d).start()
    send_low(0, red[...])

    def forward(c):
        load_wq(c).wait()

        @alone
        def _():
            term = mm(x[...], wq[c], 1, 0)
            qt[:, c] = term.astype(BF).reshape(n_row, blk, width)

    def low_part():
        load_cot.wait()
        load_ou.wait()

        @alone
        def _():
            own = tokens // n_col
            first = pl.multiple_of(mc * own, own)
            part = mm(cot[pl.ds(first, own), :], ou[...], 1, 1)
            part_all[mc] = jnp.concatenate([part, jnp.zeros((own, HD - rank), F32)], axis=1).astype(BF)

        for d in range(1, n_col):
            part_copy(d).start()

    for c in range(n_chunk):
        forward(c)
        if c == 0:
            for i in range(3, n_chunk):
                load_wq(i).start()
        if c == min(2, n_chunk - 1):
            for i in range(1, len(units)):
                load_wo(i).start()
        if c == min(1, n_chunk - 1):
            load_wo(0).start()
            load_od.start()
            load_forget.start()
        if c == min(2, n_chunk - 1):
            low_part()

    settle(ends_all.at[others], ends_sem.at[1])
    for r in range(n_row):
        same_all[r] = jnp.where(same_document(r), 1.0, 0.0).astype(BF)
        hit = place_in_document(r) == slot_f
        for h in range(4):
            sel[r, h * blk : (h + 1) * blk, :] = jnp.where(hit & (head_of == h), 1.0, 0.0).astype(BF)

    def backward(i):
        load_wo(i).wait()

        @alone
        def _():
            first, size = units[i]
            term = mm(cot[...], wo[pl.ds(first, size)], 1, 1).astype(BF)
            for k in range(size // width):
                ht[:, first // width + k] = term[:, k * width : (k + 1) * width].reshape(n_row, blk, width)

    backward(0)
    def pair_blocks(j):
        empty = jnp.zeros((blk, HD), BF)
        for r in range(n_row):
            block = kv_all[j, r * blk : (r + 1) * blk]
            bd[j, r] = jnp.concatenate(
                [jnp.concatenate([block, empty], axis=1), jnp.concatenate([empty, block], axis=1)], axis=0
            )

    def send_scores():
        wide = [mm(qt[r].reshape(n_chunk * blk, width), bd[0, r], 1, 1) for r in range(n_row)]
        for r in range(n_row):
            s_send[r] = fold(r, split_rows(wide[r])).astype(BF).reshape(n_quad, blk, 2 * blk)
        for d in range(1, n_row):
            s_copy(d).start()

    def send_prob(q):
        count = min(2, n_chunk - 2 * q)
        wide = [
            mm(ht[r, 2 * q : 2 * q + count].reshape(count * blk, width), bd[1, r], 1, 1) for r in range(n_row)
        ]
        for r in range(n_row):
            pg_send[q, r] = fold(r, split_rows(wide[r])).astype(BF)
        for d in range(1, n_row):
            pg_copy(q, d).start()

    settle(kv_recv.at[others], kv_sem.at[1])
    total = kv_send[...].astype(F32)
    for d in range(1, n_row):
        total = total + kv_recv[d].astype(F32)
    kv_all[role] = total.astype(BF)
    mate_copy.start()


    @pl.when(role == 0)
    def _():
        pair_blocks(0)
        send_scores()

    @pl.when(role == 1)
    def _():
        pair_blocks(1)
        send_prob(0)

    for i in range(1, len(units) - 1):
        backward(i)
    settle(part_all.at[pl.ds(1, n_col - 1)], part_sem.at[1])
    send_low(1, part_all[...].reshape(tokens, HD)[:, 0:rank])
    settle(kv_all.at[1 - role], mate_sem.at[1])

    @pl.when(role == 1)
    def _():
        pair_blocks(0)
        send_scores()

    @pl.when(role == 0)
    def _():
        pair_blocks(1)
        send_prob(0)

    if len(units) > 1:
        backward(len(units) - 1)

    @alone
    def _():
        for q in range(1, n_quad):
            send_prob(q)

    def sign_of(first):
        lane = lax.broadcasted_iota(jnp.int32, (blk, tokens), 1)
        sub = lax.broadcasted_iota(jnp.int32, (blk, tokens), 0)
        picked = jnp.where(lane == sub + first, forget_ref[...], 0)
        return (1 - 2 * jnp.sum(picked, axis=1, keepdims=True)).astype(F32)

    load_forget.wait()
    load_up.wait()
    load_od.wait()
    sign = sign_of(me * blk)
    ku = jnp.concatenate(
        [mm(bd[0, me], up[:, c * width : (c + 1) * width], 1, 1) for c in range(n_chunk)], axis=0
    ).astype(BF)
    vo = jnp.concatenate(
        [mm(bd[1, me], od[:, c * width : (c + 1) * width], 1, 1) for c in range(n_chunk)], axis=0
    ).astype(BF)
    same = same_document(me)
    allowed = slot_f <= place_in_document(me)
    wide = lax.broadcasted_iota(jnp.int32, (4 * blk, 2 * blk), 0)
    narrow = lax.broadcasted_iota(jnp.int32, (4 * blk, 2 * blk), 1)
    ones = jnp.where(lax.div(lax.rem(wide, 2 * blk), pack) == lax.div(narrow, pack), 1.0, 0.0).astype(BF)

    def head_sum(values):
        high = values.astype(BF)
        low = (values - high.astype(F32)).astype(BF)
        return mm(jnp.concatenate([high, low], axis=1), ones, 1, 0)

    def stack(blocks):
        return jnp.concatenate(blocks, axis=0)

    def unfold(values):
        open_ = mm(values.astype(BF), sel[me], 1, 1)
        keep = jnp.concatenate([same, same], axis=1)
        parts = [jnp.where(keep, open_[q * blk : (q + 1) * blk], 0.0) for q in range(n_quad)]
        return jnp.concatenate(parts, axis=1)[:, 0 : n_chunk * 2 * blk].astype(BF)

    def spread_low(low, narrow):
        wide = SCALE * mm(low, narrow, 1, 1)
        return fold(me, [wide[:, c * 2 * blk : (c + 1) * 2 * blk] for c in range(n_chunk)])

    in_low = sum_low(0).astype(BF)
    score_low = spread_low(in_low, ku)

    settle(s_recv.at[others], s_sem.at[1])
    total = s_send[me].astype(F32)
    for d in range(1, n_row):
        total = total + s_recv[d].astype(F32)
    total = total.reshape(n_quad * blk, 2 * blk) + score_low
    numer = jnp.where(stack([allowed] * n_quad), jnp.exp(total * inverse), 0.0)
    soft = numer / head_sum(numer)
    cat = unfold(soft)
    send_factor(1, mm(cat, vo, 1, 0))
    grad_low = (sum_low(1) * sign).astype(BF)
    prob_low = spread_low(grad_low, vo)
    send_moment(1, grad_low, cat)
    spread_factor(1)

    grads = []
    for q in range(n_quad):
        settle(pg_recv.at[q, others], pg_rs.at[q])
        total = pg_send[q, me].astype(F32)
        for d in range(1, n_row):
            total = total + pg_recv[q, d].astype(F32)
        grads.append(total * sign)
    total = stack(grads) + prob_low
    total = soft * (total - head_sum(total * soft)) * inverse
    cat = unfold(total)
    send_factor(0, mm(cat, ku, 1, 0))
    send_moment(0, in_low, cat)
    signs = [sign_of(r * blk) for r in range(n_row)]
    spread_factor(0)
    finish_moment(1)
    blocks = [(b * s).astype(BF) for b, s in zip(factor_everywhere(1), signs)]
    fac_cat[0] = jnp.concatenate(blocks, axis=0)

    @alone
    def _():
        du_ref[...] = SCALE * mm(fac_cat[0], cot[...], 0, 0)

    finish_moment(0)
    blocks = [b.astype(BF) for b in factor_everywhere(0)]
    fac_cat[1] = jnp.concatenate(blocks, axis=0)

    @alone
    def _():
        dq_ref[...] = SCALE * mm(fac_cat[1], x[...], 0, 0)

    settle(kv_recv.at[others], kv_sem.at[0])
    settle(kv_all.at[role], mate_sem.at[0])
    settle(ends_all.at[others], ends_sem.at[0])
    settle(s_recv.at[others], s_sem.at[0])
    settle(part_all.at[pl.ds(1, n_col - 1)], part_sem.at[0])
    for q in range(n_quad):
        settle(pg_recv.at[q, others], pg_ss.at[q])
    for j in range(2):
        settle(low_recv.at[j, others], low_ss.at[j])
        if direct:
            settle(fac_recv.at[j, pl.ds(1, 1)], fac_ss.at[j])
            settle(fac_every.at[j, pl.ds(1, n_row * pairs - 1)], every_ss.at[j])
        else:
            settle(fac_recv.at[j, pl.ds(1, n_col - 1)], fac_ss.at[j])
            settle(fac_all.at[j, others], all_ss.at[j])
        settle(m_all.at[j, others], m_ss.at[j])


def writer(dq, pieces, du, o_qd, o_up, o_od, o_ou, sem):
    rank = dq.shape[0]
    moves = [
        pltpu.make_async_copy(dq, o_qd, sem.at[0]),
        pltpu.make_async_copy(du, o_ou, sem.at[1]),
        pltpu.make_async_copy(pieces.at[pl.ds(0, rank)], o_up, sem.at[2]),
        pltpu.make_async_copy(pieces.at[pl.ds(rank, rank)], o_od, sem.at[3]),
    ]
    for move in moves:
        move.start()
    for move in moves:
        move.wait()


def local(
    activations,
    cotangent,
    forget,
    lengths,
    query_weight,
    key_weight,
    value_weight,
    output_projection_weight,
    query_down,
    query_up,
    output_down,
    output_up,
):
    n_row, n_col = lax.axis_size("row"), lax.axis_size("col")
    tokens, depth = activations.shape
    cols = query_weight.shape[1]
    rank = query_down.shape[1]
    blk = tokens // n_row
    width = 2 * HD
    n_chunk = cols // width
    n_quad = (n_chunk + 1) // 2
    hbm = pl.BlockSpec(memory_space=pltpu.HBM)
    vmem = pl.BlockSpec(memory_space=pltpu.VMEM)
    dma = pltpu.SemaphoreType.DMA
    dq, pieces, du = pl.pallas_call(
        functools.partial(kernel, n_row, n_col),
        out_shape=(
            jax.ShapeDtypeStruct((rank, depth), F32),
            jax.ShapeDtypeStruct((2 * rank, cols), F32),
            jax.ShapeDtypeStruct((rank, depth), F32),
        ),
        in_specs=[hbm] * 12,
        out_specs=(vmem, vmem, vmem),
        scratch_shapes=[
            pltpu.VMEM((tokens, depth), BF),
            pltpu.VMEM((tokens, depth), BF),
            pltpu.VMEM((n_chunk, depth, width), BF),
            pltpu.VMEM((depth, 2 * HD), BF),
            pltpu.VMEM((cols, depth), BF),
            pltpu.VMEM((rank, depth), BF),
            pltpu.VMEM((rank, cols), BF),
            pltpu.VMEM((rank, cols), BF),
            pltpu.VMEM((rank, depth), BF),
            pltpu.VMEM((tokens, rank), BF),
            pltpu.VMEM((n_col, tokens // n_col, HD), BF),
            pltpu.VMEM((n_row, n_chunk, blk, width), BF),
            pltpu.VMEM((n_row, n_chunk, blk, width), BF),
            pltpu.VMEM((tokens, HD), BF),
            pltpu.VMEM((n_row, tokens, HD), BF),
            pltpu.VMEM((2, tokens, HD), BF),
            pltpu.VMEM((n_row, 8, 2 * blk), F32),
            pltpu.VMEM((2, n_row, 2 * blk, 2 * HD), BF),
            pltpu.VMEM((n_row, 4 * blk, 2 * blk), BF),
            pltpu.VMEM((n_row, blk, 2 * blk), BF),
            pltpu.VMEM((n_row, n_quad, blk, 2 * blk), BF),
            pltpu.VMEM((n_row, n_quad, blk, 2 * blk), BF),
            pltpu.VMEM((n_quad, n_row, blk, 2 * blk), BF),
            pltpu.VMEM((n_quad, n_row, blk, 2 * blk), BF),
            pltpu.VMEM((2, n_row, blk // 4, 4 * rank), BF),
            pltpu.VMEM((2, n_row, blk // 4, 4 * rank), BF),
            pltpu.VMEM((2, blk // 4, 4 * rank), BF),
            pltpu.VMEM((2, n_col, blk // 4, 4 * rank), BF),
            pltpu.VMEM((2, n_row, blk // 4, 4 * rank), BF),
            pltpu.VMEM((2, n_row * n_col // 2 if n_row * n_col <= DIRECT else 1, blk // 4, 4 * rank), BF),
            pltpu.VMEM((2, n_row, n_chunk * rank, 2 * blk), BF),
            pltpu.VMEM((2, tokens, rank), BF),
            pltpu.SMEM(lengths.shape, jnp.int32),
            pltpu.VMEM((1, tokens), jnp.int32),
            dma((9,)),
            dma((n_chunk,)),
            dma((n_chunk,)),
            dma((2,)),
            dma((2,)),
            dma((2,)),
            dma((2,)),
            dma((2,)),
            dma((2,)),
            dma((2,)),
            dma((n_quad,)),
            dma((n_quad,)),
            dma((2,)),
            dma((2,)),
            dma((2,)),
            dma((2,)),
            dma((2,)),
            dma((2,)),
            dma((2,)),
            dma((2,)),
        ],
        compiler_params=pltpu.CompilerParams(
            collective_id=0, has_side_effects=True, vmem_limit_bytes=50 << 20
        ),
        name="unlearn_step",
    )(
        *(
            pltpu.with_memory_space_constraint(operand, pltpu.HBM)
            for operand in (
                lengths,
                forget.reshape(1, tokens),
                activations,
                cotangent,
                query_weight,
                key_weight,
                value_weight,
                output_projection_weight,
                query_down.T,
                query_up,
                output_down.T,
                output_up,
            )
        )
    )
    down_grad, up_grad, out_down_grad, out_up_grad = pl.pallas_call(
        writer,
        out_shape=(
            jax.ShapeDtypeStruct((rank, depth), F32),
            jax.ShapeDtypeStruct((rank, cols), F32),
            jax.ShapeDtypeStruct((rank, cols), F32),
            jax.ShapeDtypeStruct((rank, depth), F32),
        ),
        in_specs=[pl.BlockSpec(memory_space=pl.ANY)] * 3,
        out_specs=(hbm,) * 4,
        scratch_shapes=[dma((4,))],
        compiler_params=pltpu.CompilerParams(vmem_limit_bytes=1 << 20),
        name="write_outputs",
    )(dq, pieces, du)
    return down_grad.T, up_grad, out_down_grad.T, out_up_grad


def solution(mesh):
    placed = (
        P(None, "row"),
        P(None, "row"),
        P(),
        P("row", None),
        P("row", "col"),
        P("row", None),
        P("row", None),
        P("col", "row"),
        P("row", None),
        P(None, "col"),
        P("col", None),
        P(None, "row"),
    )
    return jax.shard_map(
        local,
        mesh=mesh,
        in_specs=placed,
        out_specs=(P("row", None), P(None, "col"), P("col", None), P(None, "row")),
        check_vma=False,
    )
```

```python
import functools
import math

import jax
import jax.numpy as jnp
from jax import lax
from jax.experimental import pallas as pl
from jax.experimental.pallas import tpu as pltpu
from jax.sharding import PartitionSpec as P

HD = 128
HEADS = 64
KVH = 4

SCALE = 0.5
DIRECT = 64
BF = jnp.bfloat16
F32 = jnp.float32


def mm(left, right, a, b):
    return lax.dot_general(
        left, right, (((a,), (b,)), ((), ())), preferred_element_type=F32
    )


def kernel(
    n_row,
    n_col,
    lengths_hbm,
    forget_hbm,
    x_hbm,
    cot_hbm,
    wq_hbm,
    wk_hbm,
    wv_hbm,
    wo_hbm,
    qd_hbm,
    up_hbm,
    od_hbm,
    ou_hbm,
    dq_ref,
    pieces_ref,
    du_ref,
    x,
    cot,
    wq,
    kvw,
    wo,
    qd,
    up,
    od,
    ou,
    red,
    part_all,
    qt,
    ht,
    kv_send,
    kv_recv,
    kv_all,
    ends_all,
    bd,
    sel,
    same_all,
    s_send,
    s_recv,
    pg_send,
    pg_recv,
    low_send,
    low_recv,
    fac_send,
    fac_recv,
    fac_all,
    fac_every,
    m_all,
    fac_cat,
    lengths_ref,
    forget_ref,
    load_sem,
    wq_sem,
    kv_sem,
    mate_sem,
    ends_sem,
    s_sem,
    low_ss,
    low_rs,
    part_sem,
    pg_ss,
    pg_rs,
    fac_ss,
    fac_rs,
    m_ss,
    m_rs,
    every_ss,
    every_rs,
):
    me = lax.axis_index("row")
    mc = lax.axis_index("col")
    n_chunk, depth, width = wq.shape
    n_quad = s_send.shape[1]
    rank = qd.shape[0]
    tokens = x.shape[0]
    blk = tokens // n_row
    cols = n_chunk * width
    heads = cols // HD
    pack = blk // 2
    inverse = 1.0 / math.sqrt(HD)
    group = lax.div(mc * heads, HEADS // KVH)
    group_cols = pl.ds(pl.multiple_of(group * HD, HD), HD)
    role = lax.rem(mc, 2)
    mate = mc + 1 - 2 * role
    others = pl.ds(1, n_row - 1)

    def row_peer(d):
        return lax.rem(me + d, n_row)

    def col_peer(d):
        return lax.rem(mc + d, n_col)

    def alone(body):
        pl.when(mc >= 0)(body)

    def settle(ref, sem):
        pltpu.make_async_copy(ref, ref, sem).wait()

    def load_wq(c):
        return pltpu.make_async_copy(
            wq_hbm.at[:, pl.ds(c * width, width)], wq.at[c], wq_sem.at[c]
        )

    units = [(0, min(2 * width, cols))] + [(first, width) for first in range(2 * width, cols, width)]

    def load_wo(i):
        span = pl.ds(*units[i])
        return pltpu.make_async_copy(wo_hbm.at[span], wo.at[span], wq_sem.at[i])

    load_x = pltpu.make_async_copy(x_hbm, x, load_sem.at[0])
    load_qd = pltpu.make_async_copy(qd_hbm, qd, load_sem.at[1])
    load_k = pltpu.make_async_copy(wk_hbm.at[:, group_cols], kvw.at[:, pl.ds(0, HD)], load_sem.at[2])
    load_v = pltpu.make_async_copy(wv_hbm.at[:, group_cols], kvw.at[:, pl.ds(0, HD)], load_sem.at[2])
    load_cot = pltpu.make_async_copy(cot_hbm, cot, load_sem.at[0])
    load_ou = pltpu.make_async_copy(ou_hbm, ou, load_sem.at[1])
    load_len = pltpu.make_async_copy(lengths_hbm, lengths_ref, load_sem.at[3])
    load_forget = pltpu.make_async_copy(forget_hbm, forget_ref, load_sem.at[3])
    load_up = pltpu.make_async_copy(up_hbm, up, load_sem.at[4])
    load_od = pltpu.make_async_copy(od_hbm, od, load_sem.at[2])
    load_len.start()
    load_qd.start()
    load_x.start()

    @pl.when(role == 0)
    def _():
        load_k.start()

    @pl.when(role == 1)
    def _():
        load_v.start()

    load_wq(0).start()
    load_up.start()

    barrier = pltpu.get_barrier_semaphore()

    def greet(where):
        pl.semaphore_signal(barrier, inc=1, device_id=where, device_id_type=pl.DeviceIdType.MESH)

    for d in range(1, n_row):
        greet({"row": row_peer(d)})
    for d in range(1, n_col):
        greet({"col": col_peer(d)})

    def remote(src, dst, send, recv, where):
        return pltpu.make_async_remote_copy(
            src_ref=src,
            dst_ref=dst,
            send_sem=send,
            recv_sem=recv,
            device_id=where,
            device_id_type=pl.DeviceIdType.MESH,
        )

    def ends_copy(d):
        return remote(ends_all.at[me], ends_all.at[me], ends_sem.at[0], ends_sem.at[1], {"row": row_peer(d)})

    def kv_copy(d):
        return remote(kv_send, kv_recv.at[d], kv_sem.at[0], kv_sem.at[1], {"row": row_peer(d)})

    mate_copy = remote(kv_all.at[role], kv_all.at[role], mate_sem.at[0], mate_sem.at[1], {"col": mate})

    def s_copy(d):
        p = row_peer(d)
        return remote(s_send.at[p], s_recv.at[d], s_sem.at[0], s_sem.at[1], {"row": p})

    def pg_copy(q, d):
        p = row_peer(d)
        return remote(pg_send.at[q, p], pg_recv.at[q, d], pg_ss.at[0], pg_rs.at[q], {"row": p})

    def part_copy(d):
        return remote(part_all.at[mc], part_all.at[mc], part_sem.at[0], part_sem.at[1], {"col": col_peer(d)})

    def low_copy(j, d):
        p = row_peer(d)
        return remote(low_send.at[j, p], low_recv.at[j, d], low_ss.at[0], low_rs.at[j], {"row": p})

    def fac_copy(j, d):
        return remote(fac_send.at[j], fac_recv.at[j, d], fac_ss.at[0], fac_rs.at[j], {"col": col_peer(d)})

    def all_copy(j, d):
        return remote(fac_all.at[j, me], fac_all.at[j, me], every_ss.at[0], every_rs.at[j], {"row": row_peer(d)})

    def m_copy(j, d):
        return remote(m_all.at[j, me], m_all.at[j, me], m_ss.at[0], m_rs.at[j], {"row": row_peer(d)})

    quarter = blk // 4

    def pack_rows(block):
        return jnp.concatenate([block[i * quarter : (i + 1) * quarter] for i in range(4)], axis=1)

    def unpack_rows(block):
        return jnp.concatenate([block[:, i * rank : (i + 1) * rank] for i in range(4)], axis=0)

    def send_low(j, partial):
        for r in range(n_row):
            low_send[j, r] = pack_rows(partial[r * blk : (r + 1) * blk])
        for d in range(1, n_row):
            low_copy(j, d).start()

    def sum_low(j):
        settle(low_recv.at[j, others], low_rs.at[j])
        low = low_send[j, me].astype(F32)
        for d in range(1, n_row):
            low = low + low_recv[j, d].astype(F32)
        return unpack_rows(low)

    direct = n_row * n_col <= DIRECT
    pairs = n_col // 2
    place = me * pairs + lax.div(mc, 2)

    def fac_swap(j):
        return remote(fac_send.at[j], fac_recv.at[j, 1], fac_ss.at[0], fac_rs.at[j], {"col": mate})

    def every_copy(j, a, b):
        return remote(
            fac_every.at[j, place],
            fac_every.at[j, place],
            every_ss.at[0],
            every_rs.at[j],
            {"row": row_peer(a), "col": col_peer(2 * b)},
        )

    def send_factor(j, factor):
        fac_send[j] = pack_rows(factor).astype(BF)
        if direct:
            fac_swap(j).start()
            return
        for d in range(1, n_col):
            fac_copy(j, d).start()

    def spread_factor(j):
        if direct:
            settle(fac_recv.at[j, pl.ds(1, 1)], fac_rs.at[j])
            fac_every[j, place] = (fac_send[j].astype(F32) + fac_recv[j, 1].astype(F32)).astype(BF)
            for b in [*range(1, pairs), 0]:
                for a in range(n_row):
                    if a + b > 0:
                        every_copy(j, a, b).start()
            return
        settle(fac_recv.at[j, pl.ds(1, n_col - 1)], fac_rs.at[j])
        total = fac_send[j].astype(F32)
        for d in range(1, n_col):
            total = total + fac_recv[j, d].astype(F32)
        fac_all[j, me] = total.astype(BF)
        for d in range(1, n_row):
            all_copy(j, d).start()

    def factor_everywhere(j):
        if direct:
            settle(fac_every.at[j, pl.ds(1, n_row * pairs - 1)], every_rs.at[j])
            blocks = []
            for r in range(n_row):
                total = fac_every[j, r * pairs].astype(F32)
                for c in range(1, pairs):
                    total = total + fac_every[j, r * pairs + c].astype(F32)
                blocks.append(unpack_rows(total))
            return blocks
        settle(fac_all.at[j, others], every_rs.at[j])
        blocks = []
        for r in range(n_row):
            blocks.append(unpack_rows(fac_all[j, r].astype(F32)))
        return blocks

    def send_moment(j, low, cat):
        moment = (SCALE * mm(low, cat, 0, 0)).astype(BF)
        for c in range(n_chunk):
            m_all[j, me, c * rank : (c + 1) * rank, :] = moment[:, c * 2 * blk : (c + 1) * 2 * blk]
        for d in range(1, n_row):
            m_copy(j, d).start()

    def finish_moment(j):
        settle(m_all.at[j, others], m_rs.at[j])

        @alone
        def _():
            total = mm(m_all[j, 0], bd[j, 0], 1, 0)
            for r in range(1, n_row):
                total = total + mm(m_all[j, r], bd[j, r], 1, 0)
            for c in range(n_chunk):
                pieces_ref[j * rank : (j + 1) * rank, c * width : (c + 1) * width] = total[
                    c * rank : (c + 1) * rank
                ]

    lane = lax.broadcasted_iota(jnp.int32, (blk, 2 * blk), 1)
    token_f = lax.broadcasted_iota(jnp.int32, (blk, 2 * blk), 0).astype(F32)
    key_f = lax.rem(lane, blk).astype(F32)
    slot_f = lax.rem(lane, pack).astype(F32)
    head_of = lax.div(lane, pack)

    def ends_of(r):
        return [ends_all[r, i : i + 1, :] for i in range(lengths_ref.shape[1])]

    def same_document(r):
        query_seg = jnp.zeros((blk, 2 * blk), F32)
        key_seg = jnp.zeros((blk, 2 * blk), F32)
        for end in ends_of(r):
            query_seg = query_seg + jnp.where(token_f >= end, 1.0, 0.0)
            key_seg = key_seg + jnp.where(key_f >= end, 1.0, 0.0)
        return query_seg == key_seg

    def place_in_document(r):
        start = jnp.zeros((blk, 2 * blk), F32)
        for end in ends_of(r):
            start = jnp.where(token_f >= end, end, start)
        return token_f - start

    def fold(r, parts):
        kept = [part.astype(BF) * same_all[r] for part in parts]
        rows = [jnp.concatenate(kept[i : i + 2], axis=1) for i in range(0, len(kept), 2)]
        rows = jnp.concatenate(rows, axis=0)
        return mm(rows, sel[r, 0 : rows.shape[1]], 1, 0)

    def split_rows(part):
        return [part[i * blk : (i + 1) * blk] for i in range(part.shape[0] // blk)]

    load_len.wait()
    rows8 = lax.broadcasted_iota(jnp.int32, (8, 2 * blk), 0)
    tile = jnp.zeros((8, 2 * blk), jnp.int32)
    end = 0
    for i in range(lengths_ref.shape[1]):
        end = end + lengths_ref[0, i]
        tile = jnp.where(rows8 == i, end, tile)
    ends_all[me] = tile.astype(F32)
    load_qd.wait()
    kvw[:, HD:] = jnp.concatenate([qd[...].T, jnp.zeros((depth, HD - rank), BF)], axis=1)
    load_x.wait()
    if n_chunk > 1:
        load_wq(1).start()
    load_k.wait()
    if n_chunk > 2:
        load_wq(2).start()

    @alone
    def _():
        both = mm(x[...], kvw[...], 1, 0).astype(BF)
        kv_send[...] = both[:, 0:HD]
        red[...] = both[:, HD : HD + rank]

    load_cot.start()
    load_ou.start()
    pl.semaphore_wait(barrier, n_row + n_col - 2)
    for d in range(1, n_row):
        ends_copy(d).start()
    for d in range(1, n_row):
        kv_copy(d).start()
    send_low(0, red[...])

    def forward(c):
        load_wq(c).wait()

        @alone
        def _():
            term = mm(x[...], wq[c], 1, 0)
            qt[:, c] = term.astype(BF).reshape(n_row, blk, width)

    def low_part():
        load_cot.wait()
        load_ou.wait()

        @alone
        def _():
            own = tokens // n_col
            first = pl.multiple_of(mc * own, own)
            part = mm(cot[pl.ds(first, own), :], ou[...], 1, 1)
            part_all[mc] = jnp.concatenate([part, jnp.zeros((own, HD - rank), F32)], axis=1).astype(BF)

        for d in range(1, n_col):
            part_copy(d).start()

    for c in range(n_chunk):
        forward(c)
        if c == 0:
            for i in range(3, n_chunk):
                load_wq(i).start()
        if c == min(2, n_chunk - 1):
            for i in range(1, len(units)):
                load_wo(i).start()
        if c == min(1, n_chunk - 1):
            load_wo(0).start()
            load_od.start()
            load_forget.start()
        if c == min(2, n_chunk - 1):
            low_part()

    settle(ends_all.at[others], ends_sem.at[1])
    for r in range(n_row):
        same_all[r] = jnp.where(same_document(r), 1.0, 0.0).astype(BF)
        hit = place_in_document(r) == slot_f
        for h in range(4):
            sel[r, h * blk : (h + 1) * blk, :] = jnp.where(hit & (head_of == h), 1.0, 0.0).astype(BF)

    def backward(i):
        load_wo(i).wait()

        @alone
        def _():
            first, size = units[i]
            term = mm(cot[...], wo[pl.ds(first, size)], 1, 1).astype(BF)
            for k in range(size // width):
                ht[:, first // width + k] = term[:, k * width : (k + 1) * width].reshape(n_row, blk, width)

    backward(0)
    def pair_blocks(j):
        empty = jnp.zeros((blk, HD), BF)
        for r in range(n_row):
            block = kv_all[j, r * blk : (r + 1) * blk]
            bd[j, r] = jnp.concatenate(
                [jnp.concatenate([block, empty], axis=1), jnp.concatenate([empty, block], axis=1)], axis=0
            )

    def send_scores():
        wide = [mm(qt[r].reshape(n_chunk * blk, width), bd[0, r], 1, 1) for r in range(n_row)]
        for r in range(n_row):
            s_send[r] = fold(r, split_rows(wide[r])).astype(BF).reshape(n_quad, blk, 2 * blk)
        for d in range(1, n_row):
            s_copy(d).start()

    def send_prob(q):
        count = min(2, n_chunk - 2 * q)
        wide = [
            mm(ht[r, 2 * q : 2 * q + count].reshape(count * blk, width), bd[1, r], 1, 1) for r in range(n_row)
        ]
        for r in range(n_row):
            pg_send[q, r] = fold(r, split_rows(wide[r])).astype(BF)
        for d in range(1, n_row):
            pg_copy(q, d).start()

    settle(kv_recv.at[others], kv_sem.at[1])
    total = kv_send[...].astype(F32)
    for d in range(1, n_row):
        total = total + kv_recv[d].astype(F32)
    kv_all[role] = total.astype(BF)
    mate_copy.start()


    @pl.when(role == 0)
    def _():
        pair_blocks(0)
        send_scores()

    @pl.when(role == 1)
    def _():
        pair_blocks(1)
        send_prob(0)

    for i in range(1, len(units) - 1):
        backward(i)
    settle(part_all.at[pl.ds(1, n_col - 1)], part_sem.at[1])
    send_low(1, part_all[...].reshape(tokens, HD)[:, 0:rank])
    settle(kv_all.at[1 - role], mate_sem.at[1])

    @pl.when(role == 1)
    def _():
        pair_blocks(0)
        send_scores()

    @pl.when(role == 0)
    def _():
        pair_blocks(1)
        send_prob(0)

    if len(units) > 1:
        backward(len(units) - 1)

    @alone
    def _():
        for q in range(1, n_quad):
            send_prob(q)

    def sign_of(first):
        lane = lax.broadcasted_iota(jnp.int32, (blk, tokens), 1)
        sub = lax.broadcasted_iota(jnp.int32, (blk, tokens), 0)
        picked = jnp.where(lane == sub + first, forget_ref[...], 0)
        return (1 - 2 * jnp.sum(picked, axis=1, keepdims=True)).astype(F32)

    load_forget.wait()
    load_up.wait()
    load_od.wait()
    sign = sign_of(me * blk)
    ku = jnp.concatenate(
        [mm(bd[0, me], up[:, c * width : (c + 1) * width], 1, 1) for c in range(n_chunk)], axis=0
    ).astype(BF)
    vo = jnp.concatenate(
        [mm(bd[1, me], od[:, c * width : (c + 1) * width], 1, 1) for c in range(n_chunk)], axis=0
    ).astype(BF)
    same = same_document(me)
    allowed = slot_f <= place_in_document(me)
    wide = lax.broadcasted_iota(jnp.int32, (4 * blk, 2 * blk), 0)
    narrow = lax.broadcasted_iota(jnp.int32, (4 * blk, 2 * blk), 1)
    ones = jnp.where(lax.div(lax.rem(wide, 2 * blk), pack) == lax.div(narrow, pack), 1.0, 0.0).astype(BF)

    def head_sum(values):
        high = values.astype(BF)
        low = (values - high.astype(F32)).astype(BF)
        return mm(jnp.concatenate([high, low], axis=1), ones, 1, 0)

    def stack(blocks):
        return jnp.concatenate(blocks, axis=0)

    def unfold(values):
        open_ = mm(values.astype(BF), sel[me], 1, 1)
        keep = jnp.concatenate([same, same], axis=1)
        parts = [jnp.where(keep, open_[q * blk : (q + 1) * blk], 0.0) for q in range(n_quad)]
        return jnp.concatenate(parts, axis=1)[:, 0 : n_chunk * 2 * blk].astype(BF)

    def spread_low(low, narrow):
        wide = SCALE * mm(low, narrow, 1, 1)
        return fold(me, [wide[:, c * 2 * blk : (c + 1) * 2 * blk] for c in range(n_chunk)])

    in_low = sum_low(0).astype(BF)
    score_low = spread_low(in_low, ku)

    settle(s_recv.at[others], s_sem.at[1])
    total = s_send[me].astype(F32)
    for d in range(1, n_row):
        total = total + s_recv[d].astype(F32)
    total = total.reshape(n_quad * blk, 2 * blk) + score_low
    numer = jnp.where(stack([allowed] * n_quad), jnp.exp(total * inverse), 0.0)
    soft = numer / head_sum(numer)
    cat = unfold(soft)
    send_factor(1, mm(cat, vo, 1, 0))
    grad_low = (sum_low(1) * sign).astype(BF)
    prob_low = spread_low(grad_low, vo)
    send_moment(1, grad_low, cat)
    spread_factor(1)

    grads = []
    for q in range(n_quad):
        settle(pg_recv.at[q, others], pg_rs.at[q])
        total = pg_send[q, me].astype(F32)
        for d in range(1, n_row):
            total = total + pg_recv[q, d].astype(F32)
        grads.append(total * sign)
    total = stack(grads) + prob_low
    total = soft * (total - head_sum(total * soft)) * inverse
    cat = unfold(total)
    send_factor(0, mm(cat, ku, 1, 0))
    send_moment(0, in_low, cat)
    signs = [sign_of(r * blk) for r in range(n_row)]
    spread_factor(0)
    finish_moment(1)
    blocks = [(b * s).astype(BF) for b, s in zip(factor_everywhere(1), signs)]
    fac_cat[0] = jnp.concatenate(blocks, axis=0)

    @alone
    def _():
        du_ref[...] = SCALE * mm(fac_cat[0], cot[...], 0, 0)

    finish_moment(0)
    blocks = [b.astype(BF) for b in factor_everywhere(0)]
    fac_cat[1] = jnp.concatenate(blocks, axis=0)

    @alone
    def _():
        dq_ref[...] = SCALE * mm(fac_cat[1], x[...], 0, 0)

    settle(kv_recv.at[others], kv_sem.at[0])
    settle(kv_all.at[role], mate_sem.at[0])
    settle(ends_all.at[others], ends_sem.at[0])
    settle(s_recv.at[others], s_sem.at[0])
    settle(part_all.at[pl.ds(1, n_col - 1)], part_sem.at[0])
    settle(pg_recv.at[:, others], pg_ss.at[0])
    settle(low_recv.at[:, others], low_ss.at[0])
    settle(m_all.at[:, others], m_ss.at[0])
    if direct:
        settle(fac_recv.at[:, pl.ds(1, 1)], fac_ss.at[0])
        settle(fac_every.at[:, pl.ds(1, n_row * pairs - 1)], every_ss.at[0])
    else:
        settle(fac_recv.at[:, pl.ds(1, n_col - 1)], fac_ss.at[0])
        settle(fac_all.at[:, others], every_ss.at[0])


def writer(dq, pieces, du, o_qd, o_up, o_od, o_ou, sem):
    rank = dq.shape[0]
    moves = [
        pltpu.make_async_copy(dq, o_qd, sem.at[0]),
        pltpu.make_async_copy(du, o_ou, sem.at[1]),
        pltpu.make_async_copy(pieces.at[pl.ds(0, rank)], o_up, sem.at[2]),
        pltpu.make_async_copy(pieces.at[pl.ds(rank, rank)], o_od, sem.at[3]),
    ]
    for move in moves:
        move.start()
    for move in moves:
        move.wait()


def local(
    activations,
    cotangent,
    forget,
    lengths,
    query_weight,
    key_weight,
    value_weight,
    output_projection_weight,
    query_down,
    query_up,
    output_down,
    output_up,
):
    n_row, n_col = lax.axis_size("row"), lax.axis_size("col")
    tokens, depth = activations.shape
    cols = query_weight.shape[1]
    rank = query_down.shape[1]
    blk = tokens // n_row
    width = 2 * HD
    n_chunk = cols // width
    n_quad = (n_chunk + 1) // 2
    hbm = pl.BlockSpec(memory_space=pltpu.HBM)
    vmem = pl.BlockSpec(memory_space=pltpu.VMEM)
    dma = pltpu.SemaphoreType.DMA
    dq, pieces, du = pl.pallas_call(
        functools.partial(kernel, n_row, n_col),
        out_shape=(
            jax.ShapeDtypeStruct((rank, depth), F32),
            jax.ShapeDtypeStruct((2 * rank, cols), F32),
            jax.ShapeDtypeStruct((rank, depth), F32),
        ),
        in_specs=[hbm] * 12,
        out_specs=(vmem, vmem, vmem),
        scratch_shapes=[
            pltpu.VMEM((tokens, depth), BF),
            pltpu.VMEM((tokens, depth), BF),
            pltpu.VMEM((n_chunk, depth, width), BF),
            pltpu.VMEM((depth, 2 * HD), BF),
            pltpu.VMEM((cols, depth), BF),
            pltpu.VMEM((rank, depth), BF),
            pltpu.VMEM((rank, cols), BF),
            pltpu.VMEM((rank, cols), BF),
            pltpu.VMEM((rank, depth), BF),
            pltpu.VMEM((tokens, rank), BF),
            pltpu.VMEM((n_col, tokens // n_col, HD), BF),
            pltpu.VMEM((n_row, n_chunk, blk, width), BF),
            pltpu.VMEM((n_row, n_chunk, blk, width), BF),
            pltpu.VMEM((tokens, HD), BF),
            pltpu.VMEM((n_row, tokens, HD), BF),
            pltpu.VMEM((2, tokens, HD), BF),
            pltpu.VMEM((n_row, 8, 2 * blk), F32),
            pltpu.VMEM((2, n_row, 2 * blk, 2 * HD), BF),
            pltpu.VMEM((n_row, 4 * blk, 2 * blk), BF),
            pltpu.VMEM((n_row, blk, 2 * blk), BF),
            pltpu.VMEM((n_row, n_quad, blk, 2 * blk), BF),
            pltpu.VMEM((n_row, n_quad, blk, 2 * blk), BF),
            pltpu.VMEM((n_quad, n_row, blk, 2 * blk), BF),
            pltpu.VMEM((n_quad, n_row, blk, 2 * blk), BF),
            pltpu.VMEM((2, n_row, blk // 4, 4 * rank), BF),
            pltpu.VMEM((2, n_row, blk // 4, 4 * rank), BF),
            pltpu.VMEM((2, blk // 4, 4 * rank), BF),
            pltpu.VMEM((2, n_col, blk // 4, 4 * rank), BF),
            pltpu.VMEM((2, n_row, blk // 4, 4 * rank), BF),
            pltpu.VMEM((2, n_row * n_col // 2 if n_row * n_col <= DIRECT else 1, blk // 4, 4 * rank), BF),
            pltpu.VMEM((2, n_row, n_chunk * rank, 2 * blk), BF),
            pltpu.VMEM((2, tokens, rank), BF),
            pltpu.SMEM(lengths.shape, jnp.int32),
            pltpu.VMEM((1, tokens), jnp.int32),
            dma((5,)),
            dma((n_chunk,)),
            dma((2,)),
            dma((2,)),
            dma((2,)),
            dma((2,)),
            dma((1,)),
            dma((2,)),
            dma((2,)),
            dma((1,)),
            dma((n_quad,)),
            dma((1,)),
            dma((2,)),
            dma((1,)),
            dma((2,)),
            dma((1,)),
            dma((2,)),
        ],
        compiler_params=pltpu.CompilerParams(
            collective_id=0, has_side_effects=True, vmem_limit_bytes=50 << 20
        ),
        name="unlearn_step",
    )(
        *(
            pltpu.with_memory_space_constraint(operand, pltpu.HBM)
            for operand in (
                lengths,
                forget.reshape(1, tokens),
                activations,
                cotangent,
                query_weight,
                key_weight,
                value_weight,
                output_projection_weight,
                query_down.T,
                query_up,
                output_down.T,
                output_up,
            )
        )
    )
    down_grad, up_grad, out_down_grad, out_up_grad = pl.pallas_call(
        writer,
        out_shape=(
            jax.ShapeDtypeStruct((rank, depth), F32),
            jax.ShapeDtypeStruct((rank, cols), F32),
            jax.ShapeDtypeStruct((rank, cols), F32),
            jax.ShapeDtypeStruct((rank, depth), F32),
        ),
        in_specs=[pl.BlockSpec(memory_space=pl.ANY)] * 3,
        out_specs=(hbm,) * 4,
        scratch_shapes=[dma((4,))],
        compiler_params=pltpu.CompilerParams(vmem_limit_bytes=1 << 20),
        name="write_outputs",
    )(dq, pieces, du)
    return down_grad.T, up_grad, out_down_grad.T, out_up_grad


def solution(mesh):
    placed = (
        P(None, "row"),
        P(None, "row"),
        P(),
        P("row", None),
        P("row", "col"),
        P("row", None),
        P("row", None),
        P("col", "row"),
        P("row", None),
        P(None, "col"),
        P("col", None),
        P(None, "row"),
    )
    return jax.shard_map(
        local,
        mesh=mesh,
        in_specs=placed,
        out_specs=(P("row", None), P(None, "col"), P("col", None), P(None, "row")),
        check_vma=False,
    )
```

```python
import functools
import math

import jax
import jax.numpy as jnp
from jax import lax
from jax.experimental import pallas as pl
from jax.experimental.pallas import tpu as pltpu
from jax.sharding import PartitionSpec as P

HD = 128
HEADS = 64
KVH = 4

SCALE = 0.5
DIRECT = 64
BF = jnp.bfloat16
F32 = jnp.float32


def mm(left, right, a, b):
    return lax.dot_general(
        left, right, (((a,), (b,)), ((), ())), preferred_element_type=F32
    )


def kernel(
    n_row,
    n_col,
    lengths_hbm,
    forget_hbm,
    x_hbm,
    cot_hbm,
    wq_hbm,
    wk_hbm,
    wv_hbm,
    wo_hbm,
    qd_hbm,
    up_hbm,
    od_hbm,
    ou_hbm,
    dq_ref,
    pieces_ref,
    du_ref,
    x,
    cot,
    wq,
    kvw,
    wo,
    qd,
    up,
    od,
    ou,
    red,
    part_all,
    qt,
    ht,
    kv_send,
    kv_recv,
    kv_all,
    ends_all,
    bd,
    sel,
    same_all,
    s_send,
    s_recv,
    pg_send,
    pg_recv,
    low_send,
    low_recv,
    fac_send,
    fac_recv,
    fac_all,
    fac_every,
    m_all,
    fac_cat,
    lengths_ref,
    forget_ref,
    load_sem,
    wq_sem,
    kv_sem,
    mate_sem,
    ends_sem,
    s_sem,
    low_ss,
    low_rs,
    part_sem,
    pg_ss,
    pg_rs,
    fac_ss,
    fac_rs,
    m_ss,
    m_rs,
    every_ss,
    every_rs,
    forward_sem,
):
    me = lax.axis_index("row")
    mc = lax.axis_index("col")
    n_chunk, depth, width = wq.shape
    n_quad = s_send.shape[1]
    rank = qd.shape[0]
    tokens = x.shape[0]
    blk = tokens // n_row
    cols = n_chunk * width
    heads = cols // HD
    pack = blk // 2
    inverse = 1.0 / math.sqrt(HD)
    group = lax.div(mc * heads, HEADS // KVH)
    group_cols = pl.ds(pl.multiple_of(group * HD, HD), HD)
    role = lax.rem(mc, 2)
    mate = mc + 1 - 2 * role
    others = pl.ds(1, n_row - 1)

    def row_peer(d):
        return lax.rem(me + d, n_row)

    def across(k):
        peer = 0
        for bit in range((n_row - 1).bit_length()):
            own = lax.rem(lax.div(me, 1 << bit), 2)
            peer = peer + (1 << bit) * (1 - own if (k >> bit) % 2 else own)
        return peer

    far_first = range(n_row - 1, 0, -1)

    def col_peer(d):
        return lax.rem(mc + d, n_col)

    def alone(body):
        pl.when(mc >= 0)(body)

    def settle(ref, sem):
        pltpu.make_async_copy(ref, ref, sem).wait()

    def load_wq(c):
        return pltpu.make_async_copy(
            wq_hbm.at[:, pl.ds(c * width, width)], wq.at[c], wq_sem.at[c]
        )

    units = [(first, width) for first in range(0, cols, width)]

    def load_wo(i):
        span = pl.ds(*units[i])
        return pltpu.make_async_copy(wo_hbm.at[span], wo.at[span], wq_sem.at[i])

    load_x = pltpu.make_async_copy(x_hbm, x, load_sem.at[0])
    load_qd = pltpu.make_async_copy(qd_hbm, qd, load_sem.at[1])
    load_k = pltpu.make_async_copy(wk_hbm.at[:, group_cols], kvw.at[:, pl.ds(0, HD)], load_sem.at[2])
    load_v = pltpu.make_async_copy(wv_hbm.at[:, group_cols], kvw.at[:, pl.ds(0, HD)], load_sem.at[2])
    load_cot = pltpu.make_async_copy(cot_hbm, cot, load_sem.at[0])
    load_ou = pltpu.make_async_copy(ou_hbm, ou, load_sem.at[1])
    load_len = pltpu.make_async_copy(lengths_hbm, lengths_ref, load_sem.at[3])
    load_forget = pltpu.make_async_copy(forget_hbm, forget_ref, load_sem.at[3])
    load_up = pltpu.make_async_copy(up_hbm, up, load_sem.at[4])
    load_od = pltpu.make_async_copy(od_hbm, od, load_sem.at[2])
    load_len.start()
    load_qd.start()
    load_x.start()

    @pl.when(role == 0)
    def _():
        load_k.start()

    @pl.when(role == 1)
    def _():
        load_v.start()

    load_wq(0).start()
    load_up.start()

    barrier = pltpu.get_barrier_semaphore()

    def greet(where):
        pl.semaphore_signal(barrier, inc=1, device_id=where, device_id_type=pl.DeviceIdType.MESH)

    for d in range(1, n_row):
        greet({"row": row_peer(d)})
    for d in range(1, n_col):
        greet({"col": col_peer(d)})

    def remote(src, dst, send, recv, where):
        return pltpu.make_async_remote_copy(
            src_ref=src,
            dst_ref=dst,
            send_sem=send,
            recv_sem=recv,
            device_id=where,
            device_id_type=pl.DeviceIdType.MESH,
        )

    def ends_copy(d):
        return remote(ends_all.at[me], ends_all.at[me], ends_sem.at[0], ends_sem.at[1], {"row": row_peer(d)})

    def kv_copy(d):
        return remote(kv_send, kv_recv.at[d], kv_sem.at[0], kv_sem.at[1], {"row": row_peer(d)})

    mate_copy = remote(kv_all.at[role], kv_all.at[role], mate_sem.at[0], mate_sem.at[1], {"col": mate})

    def s_copy(d):
        p = across(d)
        return remote(s_send.at[p], s_recv.at[d], s_sem.at[0], s_sem.at[1], {"row": p})

    def pg_copy(q, d):
        p = across(d)
        return remote(pg_send.at[q, p], pg_recv.at[q, d], pg_ss.at[0], pg_rs.at[q], {"row": p})

    part_copy = remote(part_all.at[role], part_all.at[role], part_sem.at[0], part_sem.at[1], {"col": mate})

    def low_copy(j, d):
        p = row_peer(d)
        return remote(low_send.at[j, p], low_recv.at[j, d], low_ss.at[0], low_rs.at[j], {"row": p})

    def fac_copy(j, d):
        return remote(fac_send.at[j], fac_recv.at[j, d], fac_ss.at[0], fac_rs.at[j], {"col": col_peer(d)})

    def all_copy(j, d):
        return remote(fac_all.at[j, me], fac_all.at[j, me], every_ss.at[0], every_rs.at[j], {"row": row_peer(d)})

    def m_copy(j, d):
        return remote(m_all.at[j, me], m_all.at[j, me], m_ss.at[0], m_rs.at[j], {"row": row_peer(d)})

    quarter = blk // 4

    def pack_rows(block):
        return jnp.concatenate([block[i * quarter : (i + 1) * quarter] for i in range(4)], axis=1)

    def unpack_rows(block):
        return jnp.concatenate([block[:, i * rank : (i + 1) * rank] for i in range(4)], axis=0)

    def send_low(j, partial):
        for r in range(n_row):
            low_send[j, r] = pack_rows(partial[r * blk : (r + 1) * blk])
        for d in range(1, n_row):
            low_copy(j, d).start()

    def sum_low(j):
        settle(low_recv.at[j, others], low_rs.at[j])
        low = low_send[j, me].astype(F32)
        for d in range(1, n_row):
            low = low + low_recv[j, d].astype(F32)
        return unpack_rows(low)

    direct = n_row * n_col <= DIRECT
    pairs = n_col // 2
    place = me * pairs + lax.div(mc, 2)

    def fac_swap(j):
        return remote(fac_send.at[j], fac_recv.at[j, 1], fac_ss.at[0], fac_rs.at[j], {"col": mate})

    def every_copy(j, a, b):
        return remote(
            fac_every.at[j, place],
            fac_every.at[j, place],
            every_ss.at[0],
            every_rs.at[j],
            {"row": row_peer(a), "col": col_peer(2 * b)},
        )

    def send_factor(j, factor):
        fac_send[j] = pack_rows(factor).astype(BF)
        if direct:

            @pl.when(role == 1 - j)
            def _():
                fac_swap(j).start()

            return
        for d in range(1, n_col):
            fac_copy(j, d).start()

    def spread_factor(j):
        if direct:

            @pl.when(role == j)
            def _():
                settle(fac_recv.at[j, pl.ds(1, 1)], fac_rs.at[j])
                fac_every[j, place] = (fac_send[j].astype(F32) + fac_recv[j, 1].astype(F32)).astype(BF)
                for b in [*range(1, pairs), 0]:
                    for a in range(n_row):
                        if a + b > 0:
                            every_copy(j, a, b).start()

            return
        settle(fac_recv.at[j, pl.ds(1, n_col - 1)], fac_rs.at[j])
        total = fac_send[j].astype(F32)
        for d in range(1, n_col):
            total = total + fac_recv[j, d].astype(F32)
        fac_all[j, me] = total.astype(BF)
        for d in range(1, n_row):
            all_copy(j, d).start()

    def factor_everywhere(j):
        settle(fac_all.at[j, others], every_rs.at[j])
        blocks = []
        for r in range(n_row):
            blocks.append(unpack_rows(fac_all[j, r].astype(F32)))
        return blocks

    def forward_copy(j):
        return remote(fac_all.at[j], fac_all.at[j], forward_sem.at[0], forward_sem.at[1], {"col": mate})

    def gather_factor(j):
        settle(fac_every.at[j, pl.ds(1, n_row * pairs - 1)], every_rs.at[j])
        for r in range(n_row):
            total = fac_every[j, r * pairs].astype(F32)
            for c in range(1, pairs):
                total = total + fac_every[j, r * pairs + c].astype(F32)
            fac_all[j, r] = total.astype(BF)
        forward_copy(j).start()

    def factor_blocks(j):
        return [unpack_rows(fac_all[j, r].astype(F32)) for r in range(n_row)]

    def send_moment(j, low, cat):
        moment = (SCALE * mm(low, cat, 0, 0)).astype(BF)
        for c in range(n_chunk):
            m_all[j, me, c * rank : (c + 1) * rank, :] = moment[:, c * 2 * blk : (c + 1) * 2 * blk]
        for d in range(1, n_row):
            m_copy(j, d).start()

    def finish_moment(j):
        settle(m_all.at[j, others], m_rs.at[j])

        @alone
        def _():
            total = mm(m_all[j, 0], bd[j, 0], 1, 0)
            for r in range(1, n_row):
                total = total + mm(m_all[j, r], bd[j, r], 1, 0)
            for c in range(n_chunk):
                pieces_ref[j * rank : (j + 1) * rank, c * width : (c + 1) * width] = total[
                    c * rank : (c + 1) * rank
                ]

    lane = lax.broadcasted_iota(jnp.int32, (blk, 2 * blk), 1)
    token_f = lax.broadcasted_iota(jnp.int32, (blk, 2 * blk), 0).astype(F32)
    key_f = lax.rem(lane, blk).astype(F32)
    slot_f = lax.rem(lane, pack).astype(F32)
    head_of = lax.div(lane, pack)

    def ends_of(r):
        return [ends_all[r, i : i + 1, :] for i in range(lengths_ref.shape[1])]

    def same_document(r):
        query_seg = jnp.zeros((blk, 2 * blk), F32)
        key_seg = jnp.zeros((blk, 2 * blk), F32)
        for end in ends_of(r):
            query_seg = query_seg + jnp.where(token_f >= end, 1.0, 0.0)
            key_seg = key_seg + jnp.where(key_f >= end, 1.0, 0.0)
        return query_seg == key_seg

    def place_in_document(r):
        start = jnp.zeros((blk, 2 * blk), F32)
        for end in ends_of(r):
            start = jnp.where(token_f >= end, end, start)
        return token_f - start

    def fold(r, parts):
        kept = [part.astype(BF) * same_all[r] for part in parts]
        rows = [jnp.concatenate(kept[i : i + 2], axis=1) for i in range(0, len(kept), 2)]
        rows = jnp.concatenate(rows, axis=0)
        return mm(rows, sel[r, 0 : rows.shape[1]], 1, 0)

    def split_rows(part):
        return [part[i * blk : (i + 1) * blk] for i in range(part.shape[0] // blk)]

    load_len.wait()
    rows8 = lax.broadcasted_iota(jnp.int32, (8, 2 * blk), 0)
    tile = jnp.zeros((8, 2 * blk), jnp.int32)
    end = 0
    for i in range(lengths_ref.shape[1]):
        end = end + lengths_ref[0, i]
        tile = jnp.where(rows8 == i, end, tile)
    ends_all[me] = tile.astype(F32)
    load_qd.wait()
    kvw[:, HD:] = jnp.concatenate([qd[...].T, jnp.zeros((depth, HD - rank), BF)], axis=1)
    load_x.wait()
    if n_chunk > 1:
        load_wq(1).start()
    load_k.wait()
    if n_chunk > 2:
        load_wq(2).start()

    @alone
    def _():
        both = mm(x[...], kvw[...], 1, 0).astype(BF)
        kv_send[...] = both[:, 0:HD]
        red[...] = both[:, HD : HD + rank]

    for c in range(3, n_chunk):
        load_wq(c).start()
    pl.semaphore_wait(barrier, n_row + n_col - 2)
    for d in range(1, n_row):
        ends_copy(d).start()
    for d in range(1, n_row):
        kv_copy(d).start()
    send_low(0, red[...])

    def forward(c):
        load_wq(c).wait()

        @alone
        def _():
            term = mm(x[...], wq[c], 1, 0)
            qt[:, c] = term.astype(BF).reshape(n_row, blk, width)

    def low_part():
        load_cot.wait()
        load_ou.wait()

        @alone
        def _():
            own = tokens // 2
            first = pl.multiple_of(role * own, own)
            part = mm(cot[pl.ds(first, own), :], ou[...], 1, 1)
            part_all[role] = jnp.concatenate([part, jnp.zeros((own, HD - rank), F32)], axis=1).astype(BF)

        part_copy.start()

    for c in range(n_chunk):
        forward(c)
        if c == 0:
            load_cot.start()
            load_ou.start()
        if c == min(1, n_chunk - 1):
            load_wo(0).start()
            load_od.start()
            load_forget.start()
        elif c > 1:
            load_wo(c - 1).start()
    low_part()
    for i in range(max(1, n_chunk - 1), len(units)):
        load_wo(i).start()

    def backward(i):
        load_wo(i).wait()

        @alone
        def _():
            first, size = units[i]
            term = mm(cot[...], wo[pl.ds(first, size)], 1, 1).astype(BF)
            for k in range(size // width):
                ht[:, first // width + k] = term[:, k * width : (k + 1) * width].reshape(n_row, blk, width)

    held = min(n_chunk, 2)
    for i in range(held):
        backward(i)
    def pair_blocks(j):
        empty = jnp.zeros((blk, HD), BF)
        for r in range(n_row):
            block = kv_all[j, r * blk : (r + 1) * blk]
            bd[j, r] = jnp.concatenate(
                [jnp.concatenate([block, empty], axis=1), jnp.concatenate([empty, block], axis=1)], axis=0
            )

    def send_scores():
        wide = [mm(qt[r].reshape(n_chunk * blk, width), bd[0, r], 1, 1) for r in range(n_row)]
        for r in range(n_row):
            s_send[r] = fold(r, split_rows(wide[r])).astype(BF).reshape(n_quad, blk, 2 * blk)
        for d in far_first:
            s_copy(d).start()

    def send_prob(q):
        count = min(2, n_chunk - 2 * q)
        wide = [
            mm(ht[r, 2 * q : 2 * q + count].reshape(count * blk, width), bd[1, r], 1, 1) for r in range(n_row)
        ]
        for r in range(n_row):
            pg_send[q, r] = fold(r, split_rows(wide[r])).astype(BF)
        for d in far_first:
            pg_copy(q, d).start()

    settle(ends_all.at[others], ends_sem.at[1])
    for r in range(n_row):
        same_all[r] = jnp.where(same_document(r), 1.0, 0.0).astype(BF)
        hit = place_in_document(r) == slot_f
        for h in range(4):
            sel[r, h * blk : (h + 1) * blk, :] = jnp.where(hit & (head_of == h), 1.0, 0.0).astype(BF)

    settle(kv_recv.at[others], kv_sem.at[1])
    total = kv_send[...].astype(F32)
    for d in range(1, n_row):
        total = total + kv_recv[d].astype(F32)
    kv_all[role] = total.astype(BF)
    mate_copy.start()


    @pl.when(role == 0)
    def _():
        pair_blocks(0)
        send_scores()

    @pl.when(role == 1)
    def _():
        pair_blocks(1)
        send_prob(0)

    settle(part_all.at[1 - role], part_sem.at[1])
    send_low(1, part_all[...].reshape(tokens, HD)[:, 0:rank])
    for i in range(held, len(units) - 1):
        backward(i)
    settle(kv_all.at[1 - role], mate_sem.at[1])

    @pl.when(role == 1)
    def _():
        pair_blocks(0)
        send_scores()

    @pl.when(role == 0)
    def _():
        pair_blocks(1)
        send_prob(0)

    if len(units) > held:
        backward(len(units) - 1)

    @alone
    def _():
        for q in range(1, n_quad):
            send_prob(q)

    def sign_of(first):
        lane = lax.broadcasted_iota(jnp.int32, (blk, tokens), 1)
        sub = lax.broadcasted_iota(jnp.int32, (blk, tokens), 0)
        picked = jnp.where(lane == sub + first, forget_ref[...], 0)
        return (1 - 2 * jnp.sum(picked, axis=1, keepdims=True)).astype(F32)

    load_forget.wait()
    load_up.wait()
    load_od.wait()
    sign = sign_of(me * blk)
    ku = jnp.concatenate(
        [mm(bd[0, me], up[:, c * width : (c + 1) * width], 1, 1) for c in range(n_chunk)], axis=0
    ).astype(BF)
    vo = jnp.concatenate(
        [mm(bd[1, me], od[:, c * width : (c + 1) * width], 1, 1) for c in range(n_chunk)], axis=0
    ).astype(BF)
    same = same_document(me)
    allowed = slot_f <= place_in_document(me)
    wide = lax.broadcasted_iota(jnp.int32, (4 * blk, 2 * blk), 0)
    narrow = lax.broadcasted_iota(jnp.int32, (4 * blk, 2 * blk), 1)
    ones = jnp.where(lax.div(lax.rem(wide, 2 * blk), pack) == lax.div(narrow, pack), 1.0, 0.0).astype(BF)

    def head_sum(values):
        high = values.astype(BF)
        low = (values - high.astype(F32)).astype(BF)
        return mm(jnp.concatenate([high, low], axis=1), ones, 1, 0)

    def stack(blocks):
        return jnp.concatenate(blocks, axis=0)

    def unfold(values):
        open_ = mm(values.astype(BF), sel[me], 1, 1)
        keep = jnp.concatenate([same, same], axis=1)
        parts = [jnp.where(keep, open_[q * blk : (q + 1) * blk], 0.0) for q in range(n_quad)]
        return jnp.concatenate(parts, axis=1)[:, 0 : n_chunk * 2 * blk].astype(BF)

    def spread_low(low, narrow):
        wide = SCALE * mm(low, narrow, 1, 1)
        return fold(me, [wide[:, c * 2 * blk : (c + 1) * 2 * blk] for c in range(n_chunk)])

    in_low = sum_low(0).astype(BF)
    score_low = spread_low(in_low, ku)

    signs = [sign_of(r * blk) for r in range(n_row)]
    grad_low = (sum_low(1) * sign).astype(BF)
    prob_low = spread_low(grad_low, vo)
    settle(s_recv.at[others], s_sem.at[1])
    total = s_send[me].astype(F32)
    for d in range(1, n_row):
        total = total + s_recv[d].astype(F32)
    total = total.reshape(n_quad * blk, 2 * blk) + score_low
    numer = jnp.where(stack([allowed] * n_quad), jnp.exp(total * inverse), 0.0)
    soft = numer / head_sum(numer)
    cat = unfold(soft)
    send_factor(1, mm(cat, vo, 1, 0))


    @pl.when(role == 0)
    def _():
        send_moment(1, grad_low, cat)


    grads = []
    for q in range(n_quad):
        settle(pg_recv.at[q, others], pg_rs.at[q])
        total = pg_send[q, me].astype(F32)
        for d in range(1, n_row):
            total = total + pg_recv[q, d].astype(F32)
        grads.append(total * sign)
    total = stack(grads) + prob_low
    total = soft * (total - head_sum(total * soft)) * inverse
    grad_cat = unfold(total)
    send_factor(0, mm(grad_cat, ku, 1, 0))
    spread_factor(1)

    @pl.when(role == 1)
    def _():
        send_moment(1, grad_low, cat)

    send_moment(0, in_low, grad_cat)
    spread_factor(0)
    finish_moment(1)
    def output_up_step(blocks):
        fac_cat[0] = jnp.concatenate([(b * s).astype(BF) for b, s in zip(blocks, signs)], axis=0)

        @alone
        def _():
            du_ref[...] = SCALE * mm(fac_cat[0], cot[...], 0, 0)

    def query_down_step(blocks):
        fac_cat[1] = jnp.concatenate([b.astype(BF) for b in blocks], axis=0)

        @alone
        def _():
            dq_ref[...] = SCALE * mm(fac_cat[1], x[...], 0, 0)

    if direct:

        @pl.when(role == 1)
        def _():
            gather_factor(1)
            output_up_step(factor_blocks(1))

        @pl.when(role == 0)
        def _():
            gather_factor(0)
            query_down_step(factor_blocks(0))

        finish_moment(0)
        settle(fac_all.at[1 - role], forward_sem.at[1])

        @pl.when(role == 1)
        def _():
            query_down_step(factor_blocks(0))

        @pl.when(role == 0)
        def _():
            output_up_step(factor_blocks(1))

    else:
        output_up_step(factor_everywhere(1))
        finish_moment(0)
        query_down_step(factor_everywhere(0))

    settle(kv_recv.at[others], kv_sem.at[0])
    settle(kv_all.at[role], mate_sem.at[0])
    settle(ends_all.at[others], ends_sem.at[0])
    settle(s_recv.at[others], s_sem.at[0])
    settle(part_all.at[role], part_sem.at[0])
    settle(pg_recv.at[:, others], pg_ss.at[0])
    settle(low_recv.at[:, others], low_ss.at[0])
    settle(m_all.at[:, others], m_ss.at[0])
    if direct:
        settle(fac_recv.at[0, pl.ds(1, 1)], fac_ss.at[0])
        settle(fac_every.at[0, pl.ds(1, n_row * pairs - 1)], every_ss.at[0])
        settle(fac_all.at[0], forward_sem.at[0])
    else:
        settle(fac_recv.at[:, pl.ds(1, n_col - 1)], fac_ss.at[0])
        settle(fac_all.at[:, others], every_ss.at[0])


def writer(dq, pieces, du, o_qd, o_up, o_od, o_ou, sem):
    rank = dq.shape[0]
    moves = [
        pltpu.make_async_copy(dq, o_qd, sem.at[0]),
        pltpu.make_async_copy(du, o_ou, sem.at[1]),
        pltpu.make_async_copy(pieces.at[pl.ds(0, rank)], o_up, sem.at[2]),
        pltpu.make_async_copy(pieces.at[pl.ds(rank, rank)], o_od, sem.at[3]),
    ]
    for move in moves:
        move.start()
    for move in moves:
        move.wait()


def local(
    activations,
    cotangent,
    forget,
    lengths,
    query_weight,
    key_weight,
    value_weight,
    output_projection_weight,
    query_down,
    query_up,
    output_down,
    output_up,
):
    n_row, n_col = lax.axis_size("row"), lax.axis_size("col")
    tokens, depth = activations.shape
    cols = query_weight.shape[1]
    rank = query_down.shape[1]
    blk = tokens // n_row
    width = 2 * HD
    n_chunk = cols // width
    n_quad = (n_chunk + 1) // 2
    hbm = pl.BlockSpec(memory_space=pltpu.HBM)
    vmem = pl.BlockSpec(memory_space=pltpu.VMEM)
    dma = pltpu.SemaphoreType.DMA
    dq, pieces, du = pl.pallas_call(
        functools.partial(kernel, n_row, n_col),
        out_shape=(
            jax.ShapeDtypeStruct((rank, depth), F32),
            jax.ShapeDtypeStruct((2 * rank, cols), F32),
            jax.ShapeDtypeStruct((rank, depth), F32),
        ),
        in_specs=[hbm] * 12,
        out_specs=(vmem, vmem, vmem),
        scratch_shapes=[
            pltpu.VMEM((tokens, depth), BF),
            pltpu.VMEM((tokens, depth), BF),
            pltpu.VMEM((n_chunk, depth, width), BF),
            pltpu.VMEM((depth, 2 * HD), BF),
            pltpu.VMEM((cols, depth), BF),
            pltpu.VMEM((rank, depth), BF),
            pltpu.VMEM((rank, cols), BF),
            pltpu.VMEM((rank, cols), BF),
            pltpu.VMEM((rank, depth), BF),
            pltpu.VMEM((tokens, rank), BF),
            pltpu.VMEM((2, tokens // 2, HD), BF),
            pltpu.VMEM((n_row, n_chunk, blk, width), BF),
            pltpu.VMEM((n_row, n_chunk, blk, width), BF),
            pltpu.VMEM((tokens, HD), BF),
            pltpu.VMEM((n_row, tokens, HD), BF),
            pltpu.VMEM((2, tokens, HD), BF),
            pltpu.VMEM((n_row, 8, 2 * blk), F32),
            pltpu.VMEM((2, n_row, 2 * blk, 2 * HD), BF),
            pltpu.VMEM((n_row, 4 * blk, 2 * blk), BF),
            pltpu.VMEM((n_row, blk, 2 * blk), BF),
            pltpu.VMEM((n_row, n_quad, blk, 2 * blk), BF),
            pltpu.VMEM((n_row, n_quad, blk, 2 * blk), BF),
            pltpu.VMEM((n_quad, n_row, blk, 2 * blk), BF),
            pltpu.VMEM((n_quad, n_row, blk, 2 * blk), BF),
            pltpu.VMEM((2, n_row, blk // 4, 4 * rank), BF),
            pltpu.VMEM((2, n_row, blk // 4, 4 * rank), BF),
            pltpu.VMEM((2, blk // 4, 4 * rank), BF),
            pltpu.VMEM((2, n_col, blk // 4, 4 * rank), BF),
            pltpu.VMEM((2, n_row, blk // 4, 4 * rank), BF),
            pltpu.VMEM((2, n_row * n_col // 2 if n_row * n_col <= DIRECT else 1, blk // 4, 4 * rank), BF),
            pltpu.VMEM((2, n_row, n_chunk * rank, 2 * blk), BF),
            pltpu.VMEM((2, tokens, rank), BF),
            pltpu.SMEM(lengths.shape, jnp.int32),
            pltpu.VMEM((1, tokens), jnp.int32),
            dma((5,)),
            dma((n_chunk,)),
            dma((2,)),
            dma((2,)),
            dma((2,)),
            dma((2,)),
            dma((1,)),
            dma((2,)),
            dma((2,)),
            dma((1,)),
            dma((n_quad,)),
            dma((1,)),
            dma((2,)),
            dma((1,)),
            dma((2,)),
            dma((1,)),
            dma((2,)),
            dma((2,)),
        ],
        compiler_params=pltpu.CompilerParams(
            collective_id=0, has_side_effects=True, vmem_limit_bytes=50 << 20
        ),
        name="unlearn_step",
    )(
        *(
            pltpu.with_memory_space_constraint(operand, pltpu.HBM)
            for operand in (
                lengths,
                forget.reshape(1, tokens),
                activations,
                cotangent,
                query_weight,
                key_weight,
                value_weight,
                output_projection_weight,
                query_down.T,
                query_up,
                output_down.T,
                output_up,
            )
        )
    )
    down_grad, up_grad, out_down_grad, out_up_grad = pl.pallas_call(
        writer,
        out_shape=(
            jax.ShapeDtypeStruct((rank, depth), F32),
            jax.ShapeDtypeStruct((rank, cols), F32),
            jax.ShapeDtypeStruct((rank, cols), F32),
            jax.ShapeDtypeStruct((rank, depth), F32),
        ),
        in_specs=[pl.BlockSpec(memory_space=pl.ANY)] * 3,
        out_specs=(hbm,) * 4,
        scratch_shapes=[dma((4,))],
        compiler_params=pltpu.CompilerParams(vmem_limit_bytes=1 << 20),
        name="write_outputs",
    )(dq, pieces, du)
    return down_grad.T, up_grad, out_down_grad.T, out_up_grad


def solution(mesh):
    placed = (
        P(None, "row"),
        P(None, "row"),
        P(),
        P("row", None),
        P("row", "col"),
        P("row", None),
        P("row", None),
        P("col", "row"),
        P("row", None),
        P(None, "col"),
        P("col", None),
        P(None, "row"),
    )
    return jax.shard_map(
        local,
        mesh=mesh,
        in_specs=placed,
        out_specs=(P("row", None), P(None, "col"), P("col", None), P(None, "row")),
        check_vma=False,
    )
```
